32 devices in a mesh: dp: 16 (over z, y, x), tensor: 2 (over core).
Axes of the slice: x: 2, y: 2, z: 4, core: 2. Of those that a mesh axis runs over, the one named last changes fastest.
Arguments:
- tokens: bfloat16 [16, 2048, 512], P('dp', 'tensor'), may hold values from -6 to 6
- cotangent: bfloat16 [16, 2048, 512], P('dp', 'tensor'), may hold values from -6 to 6
- span_ids: int32 [16, 8, 256], P('dp'), may hold values from 0 to 1, never falling along the last dimension, each value on 1 to 192 neighbouring positions
- gain_one: float32 [512], replicated, may hold values from 0.25 to 1.75
- w_qkv: bfloat16 [512, 3, 512], P('dp', None, 'tensor'), may hold values from -0.25 to 0.25
- w_out: bfloat16 [512, 512], P('tensor', 'dp'), may hold values from -1 to 1
- b_out: float32 [512], replicated, may hold values from -3 to 3
- gain_two: float32 [512], replicated, may hold values from 0.25 to 1.75
- w_up: bfloat16 [512, 2048], P('dp', 'tensor'), may hold values from -0.25 to 0.25
- b_up: float32 [2048], P('tensor'), may hold values from -3 to 3
- w_down: bfloat16 [2048, 512], P('tensor', 'dp'), may hold values from -0.125 to 0.125
- b_down: float32 [512], replicated, may hold values from -3 to 3
Outputs:
- result: bfloat16 [16, 2048, 512], P('dp', 'tensor')
- d_tokens: bfloat16 [16, 2048, 512], P('dp', 'tensor')
- d_gain_one: float32 [512], replicated
- d_w_qkv: float32 [512, 3, 512], P('dp', None, 'tensor')
- d_w_out: float32 [512, 512], P('tensor', 'dp')
- d_b_out: float32 [512], replicated
- d_gain_two: float32 [512], replicated
- d_w_up: float32 [512, 2048], P('dp', 'tensor')
- d_b_up: float32 [2048], replicated
- d_w_down: float32 [2048, 512], P('tensor', 'dp')
- d_b_down: float32 [512], replicated
The draws below stay inside these ranges and needn't reach their ends.
Inputs may be any that keep to these rules, and one draw needn't show every extreme that they name: `span_ids`: within each block of 256 positions the span numbers never fall and each of the 2 spans holds 1 to 192 positions.
All inputs are finite; a program needn't handle non-finite values.
Results may differ from the reference program's by a relative error of at most 0.014.
Values may be sent and summed in bfloat16 or wider, within the bound.
A program may use at most 128 MiB of HBM per device.

```python
import math
import jax
import jax.numpy as jnp
import numpy as np
from jax import lax

D = 512
HEADS = 8
HD = 64
FF = 2048
BLK = 256
SEQ = 2048
SPB = 2
MOST = 192
NBLK = 8
NSEQ = 16
TOKENS = 32768


def strengthened(array, stream_key, source, target, blocks, factor):
    owner, partner = [(jnp.arange(array.shape[position]) // (array.shape[position] // blocks)).reshape([-1 if axis == position else 1 for axis in range(array.ndim)]) for position in (source, target)]
    chosen = jax.random.permutation(stream_key, blocks)[partner]
    strong = (owner == chosen) | (owner == (partner + blocks // 2) % blocks)
    return jnp.where(strong, factor * array, array)


def block_levels(key, shape, cuts, smallest, high):
    level, own = 1.0, jax.random.fold_in(key, 6)
    for position, shards_of in cuts:
        heights = jnp.exp(jax.random.uniform(jax.random.fold_in(own, position), (shards_of,), jnp.float32, smallest / len(cuts), high / len(cuts)))
        level = level * jnp.repeat(heights, shape[position] // shards_of).reshape([-1 if axis == position else 1 for axis in range(len(shape))])
    return level


def length_profile(count, total, limit, skew):
    weights = [(1 << 20) // math.isqrt(rank ** skew) + 1 for rank in range(2, count + 1)]
    rest, holding = total - limit - (count - 1), [1] * (count - 1)
    while rest > 0:
        free = [i for i in range(count - 1) if holding[i] < limit]
        mass, left = sum([weights[i] for i in free]), rest
        for i in free:
            more = min(limit - holding[i], max(1, left * weights[i] // mass), rest)
            holding[i] = holding[i] + more
            rest = rest - more
    return np.array([limit] + holding)


def uneven_parts(rng, amount, total, bound, skew):
    if amount == 2:
        one = jax.random.randint(rng, (), max(1, total - bound), min(bound, total - 1) + 1)
        return jnp.stack([one, total - one])
    tallies = jnp.asarray(length_profile(amount, total, bound, skew), jnp.int32)
    twos = (amount - 1) // 2
    source_of, taker = tallies[1:1 + 2 * twos:2], tallies[2:2 + 2 * twos:2]
    margin = jnp.minimum(source_of - 1, bound - taker)
    passed = jax.random.randint(jax.random.fold_in(rng, 1), (twos,), 0, 1 << 20) % (margin + 1)
    tallies = tallies.at[1:1 + 2 * twos:2].set(source_of - passed).at[2:2 + 2 * twos:2].set(taker + passed)
    return tallies[jax.random.permutation(jax.random.fold_in(rng, 2), amount)]


def scatter_about(key, shape, scale, reach, cuts=(), kind=jnp.bfloat16):
    drawn = jax.random.normal(key, shape, jnp.float32) * scale
    if len(cuts) > 0:
        drawn = block_levels(key, shape, cuts, -0.22, 0.18) * drawn
    return jnp.clip(drawn, min=-reach, max=reach).astype(kind)


def heavy_noise(stream_key, extent, width, most, shards, heavy, kind=jnp.bfloat16):
    drawn = width * jax.random.normal(stream_key, extent, jnp.float32)
    if shards:
        drawn = drawn * block_levels(stream_key, extent, shards, -0.22, 0.18)
    return jnp.clip(strengthened(drawn, jax.random.fold_in(stream_key, 3), *heavy), -most, most).astype(kind)


def setup_inputs(seed: int = 0) -> dict:
    seeds = jax.random.split(jax.random.key(seed), 13)
    return {
        "tokens": heavy_noise(seeds[0], (NSEQ, SEQ, D), 1.0, 6.0, ((0, 16), (1, 2)), (0, 2, 16, 2.0)),
        "cotangent": heavy_noise(seeds[1], (NSEQ, SEQ, D), 1.0, 6.0, ((0, 16), (1, 2)), (0, 2, 16, 2.0)),
        "span_ids": jax.vmap(lambda own: jnp.searchsorted(jnp.cumsum(uneven_parts(own, SPB, BLK, MOST, 0)), jnp.arange(BLK), side="right"))(jax.random.split(seeds[2], NSEQ * NBLK)).reshape((NSEQ, NBLK, BLK)).astype(jnp.int32),
        "gain_one": jnp.clip(1.0 + 0.15 * jax.random.normal(seeds[3], (D,), jnp.float32), 0.25, 1.75),
        "w_qkv": scatter_about(seeds[4], (D, 3, D), D ** -0.5, 0.25, ((0, 16), (2, 2))),
        "w_out": scatter_about(seeds[5], (D, D), (D // 16) ** -0.5, 1.0, ((0, 2), (1, 16))),
        "b_out": scatter_about(seeds[6], (D,), 0.5, 3.0, (), jnp.float32),
        "gain_two": jnp.clip(1.0 + 0.15 * jax.random.normal(seeds[7], (D,), jnp.float32), 0.25, 1.75),
        "w_up": scatter_about(seeds[8], (D, FF), D ** -0.5, 0.25, ((0, 16), (1, 2))),
        "b_up": scatter_about(seeds[9], (FF,), 0.5, 3.0, ((0, 2),), jnp.float32),
        "w_down": scatter_about(seeds[10], (FF, D), FF ** -0.5, 0.125, ((0, 2), (1, 16))),
        "b_down": scatter_about(seeds[11], (D,), 0.5, 3.0, (), jnp.float32),
    }


@jax.custom_vjp
def low(v):
    return lax.optimization_barrier(v.astype(jnp.bfloat16)).astype(jnp.float32)

@jax.custom_vjp
def low_back(v):
    return v

def low_keep(v):
    return (low(v), None)

def low_pass(kept, grad):
    return (grad,)

def back_keep(v):
    return (v, None)

def back_low(kept, grad):
    return (low(grad),)
low.defvjp(low_keep, low_pass)
low_back.defvjp(back_keep, back_low)
epsilon = 1e-05
masked = -1e+30
highest = lax.Precision.HIGHEST

def normalize(values, gain_vec):
    centre = values - lax.optimization_barrier(jnp.mean(values, axis=-1, keepdims=True))
    spread = lax.optimization_barrier(jnp.mean(centre * centre, axis=-1, keepdims=True))
    return centre * lax.rsqrt(spread + epsilon) * gain_vec

def rounded_both(values):
    return low(low_back(values))

def one_sequence(incoming, span_rows, gain_one, w_qkv, w_out, b_out, gain_two, w_up, b_up, w_down, b_down):
    blocks = span_rows.shape[0]
    length = blocks * BLK
    scaling = 1.0 / math.sqrt(HD)
    normed = low(normalize(incoming, gain_one))
    projected = rounded_both(jnp.dot(normed, w_qkv.reshape(D, 3 * D), precision=highest))
    projected = projected.reshape(blocks, BLK, 3, HEADS, HD)
    queries = projected[:, :, 0]
    key_rows = projected[:, :, 1]
    value_rows = projected[:, :, 2]
    member = (span_rows[:, :, None] == jnp.arange(SPB, dtype=jnp.int32)[None, None, :]).astype(jnp.float32)
    counts = lax.optimization_barrier(jnp.sum(member, axis=1))
    key_sum = low(jnp.einsum('bjm,bjhe->bmhe', member, key_rows, precision=highest) / counts[:, :, None, None])
    value_sum = low(jnp.einsum('bjm,bjhe->bmhe', member, value_rows, precision=highest) / counts[:, :, None, None])
    key_sum = key_sum.reshape(blocks * SPB, HEADS, HD)
    value_sum = value_sum.reshape(blocks * SPB, HEADS, HD)
    near_scores = low_back(jnp.einsum('bihe,bjhe->bhij', queries, key_rows, precision=highest) * scaling)
    far_scores = low_back(jnp.einsum('bihe,che->bhic', queries, key_sum, precision=highest) * scaling + jnp.log(counts).reshape(-1))
    allowed = jnp.arange(blocks)[:, None] > (jnp.arange(blocks * SPB) // SPB)[None, :]
    far_scores = jnp.where(allowed[:, None, None, :], far_scores, masked)
    joined = jnp.concatenate([near_scores, far_scores], axis=-1)
    largest = lax.optimization_barrier(jnp.max(joined, axis=-1, keepdims=True))
    exps = jnp.exp(joined - largest)
    probs = low(exps / lax.optimization_barrier(jnp.sum(exps, axis=-1, keepdims=True)))
    attended = jnp.einsum('bhij,bjhe->bihe', probs[..., :BLK], value_rows, precision=highest)
    attended = attended + jnp.einsum('bhic,che->bihe', probs[..., BLK:], value_sum, precision=highest)
    attended = rounded_both(attended.reshape(length, D))
    branch = low_back(jnp.dot(attended, w_out, precision=highest) + b_out)
    middle = incoming + branch
    second = low(normalize(middle, gain_two))
    before_gelu = low_back(jnp.dot(second, w_up, precision=highest) + b_up)
    hidden = low(jax.nn.gelu(before_gelu))
    branch_two = low_back(jnp.dot(hidden, w_down, precision=highest) + b_down)
    return middle + branch_two

def reference(tokens, cotangent, span_ids, gain_one, w_qkv, w_out, b_out, gain_two, w_up, b_up, w_down, b_down):
    weights = tuple((w.astype(jnp.float32) for w in (gain_one, w_qkv, w_out, b_out, gain_two, w_up, b_up, w_down, b_down)))
    incoming = tokens.astype(jnp.float32)
    checked = jax.checkpoint(one_sequence)

    def forward(values, *params):
        return lax.map(lambda pieces: checked(pieces[0], pieces[1], *params), (values, span_ids))
    output, pullback = jax.vjp(forward, incoming, *weights)
    grads = pullback(cotangent.astype(jnp.float32))
    factor = 1.0 / math.sqrt(TOKENS)
    return (output.astype(jnp.bfloat16), grads[0].astype(jnp.bfloat16), grads[1] * factor, grads[2] * factor, grads[3] * factor, grads[4] * factor, grads[5] * factor, grads[6] * factor, grads[7] * factor, grads[8] * factor, grads[9] * factor)
```

```python
import functools
import math

import jax
import jax.numpy as jnp
from jax import lax
from jax.experimental import pallas as pl
from jax.experimental.pallas import tpu as pltpu
from jax.sharding import PartitionSpec as P

HD = 64
BLK = 256
EPS = 1e-05
MASKED = -1e30
Z = 4
YX = 4
GROUPS = Z * YX
F32 = jnp.float32
BF = jnp.bfloat16
MESH = pl.DeviceIdType.MESH


def dot(a, b, ca, cb):
    return lax.dot_general(a, b, (((ca,), (cb,)), ((), ())), preferred_element_type=F32)


def nn(a, b):
    return dot(a, b, 1, 0)


def nt(a, b):
    return dot(a, b, 1, 1)


def tn(a, b):
    return dot(a, b, 0, 0)


def iota(shape, axis):
    return lax.broadcasted_iota(jnp.int32, shape, axis)


def unit_rows(values):
    centre = values - jnp.mean(values, axis=-1, keepdims=True)
    spread = jnp.mean(centre * centre, axis=-1, keepdims=True)
    inverse = lax.rsqrt(spread + EPS)
    return centre * inverse, inverse


def eight(values):
    return jnp.sum(values.reshape(values.shape[0] // 8, 8, values.shape[1]), axis=0)


class Sizes:
    pass


def kernel(s, *refs):
    (tok, cot, span, gain1, gain2, bout, bdown, bup_own, shard) = refs[:9]
    (res, dtok, gpack, o_gain1, o_gain2, o_bout, o_bdown, o_bup) = refs[9:17]
    (W, G, R0, R1, R2, R3, H1, H1T, QKV, PT, PF, O, MID, H2, H2T, COTT, HID, GI, GB, GBT,
     BUP, KSV, KB, VB, DKS, DVS, DSV, DSVR, SHARE, SPC, M8, BUACC, ACC, SM, SMR,
     ag_s, ag_r, rs_s, rs_r, sx_s, sx_r) = refs[17:]
    D, H2W, F2, rows_n, NB = s.D, s.H2W, s.F2, s.rows, s.NB
    QW = 3 * H2W
    C_OUT, C_UP, C_DN = QW, QW + H2W, QW + H2W + F2
    d = lax.axis_index("dp")
    t = lax.axis_index("tensor")
    g = d // s.sub
    z = g // YX
    yx = g % YX
    rest = d % s.sub
    b2 = 2 - t
    b3 = 1 + t

    def at(zz, q):
        return ((zz * YX + q) * s.sub + rest, t)

    def flip(q, bit):
        y_bit, x_bit = q // 2, q % 2
        return jnp.where(bit == 2, (1 - y_bit) * 2 + x_bit, y_bit * 2 + 1 - x_bit)

    yx2 = flip(yx, b2)
    yx3 = flip(yx, b3)
    yx23 = 3 - yx
    pair = (d, 1 - t)
    peer2 = at(z, yx2)
    peer3 = at(z, yx3)
    zpeers = [at((z + k) % Z, yx) for k in range(1, Z)]

    barrier = pltpu.get_barrier_semaphore()
    for who in [pair, peer2, peer3] + zpeers:
        pl.semaphore_signal(barrier, inc=1, device_id=who, device_id_type=MESH)

    W[t, z, yx] = shard[...]
    BUP[t] = jnp.broadcast_to(bup_own[...], (8, F2))

    pl.semaphore_wait(barrier, 3 + Z - 1)

    def remote(src, dst, ss, rs, who):
        return pltpu.make_async_remote_copy(
            src_ref=src, dst_ref=dst, send_sem=ss, recv_sem=rs, device_id=who, device_id_type=MESH
        )

    chunks = s.ag_chunks

    def ag_copy(c, kind):
        lo, n = chunks[c]
        cols = pl.ds(lo, n)
        if kind < 3:
            window, who = W.at[t, z, yx, :, cols], zpeers[kind]
        else:
            group, who = {
                3: (yx, peer2),
                4: (yx, peer3),
                5: (yx2, peer3),
                6: (yx, pair),
                7: (yx2, pair),
                8: (yx3, pair),
                9: (yx23, pair),
            }[kind]
            window = W.at[t, :, group, :, cols]
        return remote(window, window, ag_s.at[c, kind], ag_r.at[c, kind], who)

    def ag_recv(c, kind):
        lo, n = chunks[c]
        cols = pl.ds(lo, n)
        if kind < 3:
            window = W.at[t, (z + Z - 1 - kind) % Z, yx, :, cols]
        elif kind < 6:
            window = W.at[t, :, {3: yx2, 4: yx3, 5: yx23}[kind], :, cols]
        else:
            window = W.at[1 - t, :, {6: yx, 7: yx2, 8: yx3, 9: yx23}[kind], :, cols]
        remote(window, window, ag_s.at[c, kind], ag_r.at[c, kind], pair).wait_recv()

    def ag_start(c, kinds):
        for kind in kinds:
            ag_copy(c, kind).start()

    def ag0(c):
        ag_start(c, (0, 1, 2))

    def ag1(c):
        for kind in (0, 1, 2):
            ag_recv(c, kind)
        ag_start(c, (3, 4, 6))

    def ag2(c):
        ag_recv(c, 3)
        ag_start(c, (5, 7))

    def ag3(c):
        ag_recv(c, 4)
        ag_start(c, (8,))
        ag_recv(c, 5)
        ag_start(c, (9,))

    def ag4(c):
        for kind in (6, 7, 8, 9):
            ag_recv(c, kind)

    def small_copy(i, src, dst, who):
        return remote(src, dst, sx_s.at[i], sx_r.at[i], who)

    for c in range(len(chunks)):
        ag0(c)
    bup_copy = small_copy(0, BUP.at[t], BUP.at[t], pair)
    bup_copy.start()

    def wl(half, lo, n):
        return W[half, :, :, :, pl.ds(lo, n)].reshape(D, n)

    def rows_of(b):
        return pl.ds(pl.multiple_of(b * BLK, BLK), BLK)

    def norm_one(b, _):
        r = rows_of(b)
        unit, _inv = unit_rows(tok[r, :].astype(F32))
        low = (unit * gain1[...]).astype(BF)
        H1[r, :] = low
        H1T[:, r] = low.T
        COTT[:, r] = cot[r, :].T
        return 0

    lax.fori_loop(0, NB, norm_one, 0)

    half_rows = iota((8, BLK), 0)
    for b in range(NB):
        line = span[pl.ds(t * NB + b, 1), :]
        belongs = jnp.logical_and(half_rows // NB == line, half_rows % NB == b)
        M8[:, b * BLK:(b + 1) * BLK] = belongs.astype(F32)
    SPC[...] = jnp.concatenate([span[...].astype(F32), jnp.zeros((120, BLK), F32)], axis=0).T
    zeros_in = (span[...] == 0).astype(F32)
    ones_in = (span[...] == 1).astype(F32)
    n_zero = jnp.sum(zeros_in, axis=1, keepdims=True)
    n_one = jnp.sum(ones_in, axis=1, keepdims=True)
    counts = jnp.concatenate(
        [n_zero[:NB], n_one[:NB], n_zero[NB:2 * NB], n_one[NB:2 * NB]], axis=0
    )
    log_counts = jnp.concatenate([jnp.log(counts)] * 4, axis=0)
    own_counts = jnp.sum(M8[...], axis=1, keepdims=True)
    code = iota((64, 1), 0) % 16
    block_of = (code // 8) * NB + code % NB

    BUACC[...] = jnp.zeros_like(BUACC)
    ACC[...] = jnp.zeros_like(ACC)
    DKS[...] = jnp.zeros_like(DKS)
    DVS[...] = jnp.zeros_like(DVS)

    ag1(0)
    ag2(0)
    ag1(1)
    ag3(0)
    ag4(0)

    q_scale = jnp.where(iota((1, QW), 1) < H2W, 1.0 / math.sqrt(HD), 1.0).astype(F32)

    def project(i, _):
        b, half = i // 2, i % 2
        r = rows_of(b)
        y = nn(H1[r, :], wl(half, 0, QW)) * q_scale
        QKV[half, r, :] = y.astype(BF)
        return 0

    lax.fori_loop(0, 2 * NB, project, 0)
    ag2(1)

    member_low = jnp.concatenate([M8[...], M8[...]], axis=0).astype(BF)
    for half in range(2):
        sums = nn(member_low, QKV[half, :, H2W:])[:8]
        means = (sums / own_counts).astype(BF).astype(F32)
        KSV[t, :, pl.ds(half * 2 * H2W, 2 * H2W)] = means
    ksv_copy = small_copy(1, KSV.at[t], KSV.at[t], pair)
    ksv_copy.start()
    ag3(1)
    small_copy(1, KSV.at[1 - t], KSV.at[1 - t], pair).wait_recv()
    diagonal = iota((64, H2W), 0) // 16 == iota((64, H2W), 1) // HD
    everything = KSV[...].reshape(16, 4 * H2W)
    for half in range(2):
        for kind, out in ((0, KB), (1, VB)):
            lo = (2 * half + kind) * H2W
            tiled = jnp.concatenate([everything[:, lo:lo + H2W]] * 4, axis=0)
            out[half] = jnp.where(diagonal, tiled, 0.0).astype(BF)

    even = iota((BLK, 128), 1) < HD

    def head_only(values, e):
        return jnp.where(even if e == 0 else jnp.logical_not(even), values, jnp.zeros_like(values))

    def attend(i, _):
        b, half = i // 2, i % 2
        r = rows_of(b)
        q = QKV[half, r, 0:H2W]
        far = nt(KB[half], q) + log_counts
        far = jnp.where(block_of < t * NB + b, far, MASKED)
        parts, far_parts = [], []
        for pr in range(2):
            lanes = slice(pr * 128, (pr + 1) * 128)
            q2 = q[:, lanes]
            k2 = QKV[half, r, H2W + pr * 128:H2W + (pr + 1) * 128]
            v2 = QKV[half, r, 2 * H2W + pr * 128:2 * H2W + (pr + 1) * 128]
            both = []
            for e in range(2):
                hl = 2 * pr + e
                near = nt(k2, head_only(q2, e))
                sf = far[16 * hl:16 * hl + 16]
                largest = jnp.maximum(
                    jnp.max(near, axis=0, keepdims=True), jnp.max(sf, axis=0, keepdims=True)
                )
                pn = jnp.exp(near - largest)
                pf = jnp.exp(sf - largest)
                total = jnp.sum(pn, axis=0, keepdims=True) + jnp.sum(pf, axis=0, keepdims=True)
                inv = 1.0 / total
                pn = (pn * inv).astype(BF)
                PT[half, b, hl] = pn
                far_parts.append(pf * inv)
                both.append(tn(pn, v2))
            parts.append(jnp.where(even, both[0], both[1]))
        pf_all = jnp.concatenate(far_parts, axis=0).astype(BF)
        PF[half, b] = pf_all
        out = jnp.concatenate(parts, axis=1) + tn(pf_all, VB[half])
        O[half, r, :] = out.astype(BF)
        for when, todo in s.fwd_slots:
            @pl.when(i == when)
            def _():
                for name, c in todo:
                    {"1": ag1, "2": ag2, "3": ag3, "4": ag4}[name](c)
        return 0

    lax.fori_loop(0, 2 * NB, attend, 0)

    small_copy(0, BUP.at[1 - t], BUP.at[1 - t], pair).wait_recv()

    def out_proj(b, _):
        r = rows_of(b)
        branch = nt(O[0, r, :], wl(0, C_OUT, H2W)) + nt(O[1, r, :], wl(1, C_OUT, H2W))
        middle = tok[r, :].astype(F32) + (branch + bout[...])
        MID[r, :] = middle
        unit, _inv = unit_rows(middle)
        low = (unit * gain2[...]).astype(BF)
        H2[r, :] = low
        H2T[:, r] = low.T
        return 0

    lax.fori_loop(0, NB, out_proj, 0)

    for name, c in s.tail_slots:
        {"1": ag1, "2": ag2, "3": ag3, "4": ag4}[name](c)

    FC = 512
    NFC = F2 // FC
    c0 = math.sqrt(2.0 / math.pi)
    c1 = c0 * 0.044715

    def feed(i, _):
        b = i // (2 * NFC)
        half = (i // NFC) % 2
        fc = pl.multiple_of((i % NFC) * FC, FC)
        r = rows_of(b)
        x = nn(H2[r, :], wl(half, pl.multiple_of(C_UP + fc, FC), FC)) + BUP[half, 0:1, pl.ds(fc, FC)]
        gh = nn(cot[r, :], wl(half, pl.multiple_of(C_DN + fc, FC), FC))
        sq = x * x
        th = jnp.tanh(x * (c0 + c1 * sq))
        up = 0.5 + 0.5 * th
        HID[half, r, pl.ds(fc, FC)] = (x * up).astype(BF)
        slope = up + (0.5 * x) * (1.0 - th * th) * (c0 + (3.0 * c1) * sq)
        gi = gh * slope
        GI[half, r, pl.ds(fc, FC)] = gi.astype(BF)
        BUACC[half, :, pl.ds(fc, FC)] += eight(gi)
        return 0

    lax.fori_loop(0, 2 * NB * NFC, feed, 0)

    def feed_back(b, _):
        r = rows_of(b)
        down = nt(HID[0, r, :], wl(0, C_DN, F2)) + nt(HID[1, r, :], wl(1, C_DN, F2))
        middle = MID[r, :]
        res[r, :] = (middle + (down + bdown[...])).astype(BF)
        g2 = nt(GI[0, r, :], wl(0, C_UP, F2)) + nt(GI[1, r, :], wl(1, C_UP, F2))
        unit, inverse = unit_rows(middle)
        e = g2 * gain2[...]
        m1 = jnp.mean(e, axis=-1, keepdims=True)
        m2 = jnp.mean(e * unit, axis=-1, keepdims=True)
        grad_out = cot[r, :].astype(F32)
        mid = grad_out + inverse * (e - m1 - unit * m2)
        MID[r, :] = mid
        low = mid.astype(BF)
        GB[r, :] = low
        GBT[:, r] = low.T
        ACC[1] += eight(g2 * unit)
        ACC[2] += eight(mid)
        ACC[3] += eight(grad_out)
        return 0

    lax.fori_loop(0, NB, feed_back, 0)

    rchunks = s.rs_chunks

    def rs_copy(c, kind):
        lo, n = rchunks[c]
        cols = pl.ds(lo, n)
        if kind == 0:
            src, dst, who = G.at[1 - t, :, :, :, cols], R0.at[:, :, :, cols], pair
        elif kind == 1:
            src, dst, who = G.at[t, :, yx3, :, cols], R1.at[0, :, :, cols], peer3
        elif kind == 2:
            src, dst, who = G.at[t, :, yx23, :, cols], R1.at[1, :, :, cols], peer3
        elif kind == 3:
            src, dst, who = G.at[t, :, yx2, :, cols], R2.at[:, :, cols], peer2
        else:
            k = kind - 3
            src, dst, who = G.at[t, (z + k) % Z, yx, :, cols], R3.at[k - 1, :, cols], zpeers[k - 1]
        return remote(src, dst, rs_s.at[c, kind], rs_r.at[c, kind], who)

    def rs0(c):
        rs_copy(c, 0).start()

    def rs1(c):
        lo, n = rchunks[c]
        rs_copy(c, 0).wait_recv()
        cols = pl.ds(lo, n)

        def add(q):
            for zz in range(Z):
                G[t, zz, q, :, cols] = (
                    G[t, zz, q, :, cols].astype(F32) + R0[zz, q, :, cols].astype(F32)
                ).astype(BF)

        add(yx23)
        rs_copy(c, 2).start()
        add(yx3)
        rs_copy(c, 1).start()
        add(yx2)
        add(yx)

    def rs2(c):
        lo, n = rchunks[c]
        cols = pl.ds(lo, n)

        def add(q, j):
            for zz in range(Z):
                G[t, zz, q, :, cols] = (
                    G[t, zz, q, :, cols].astype(F32) + R1[j, zz, :, cols].astype(F32)
                ).astype(BF)

        rs_copy(c, 2).wait_recv()
        add(yx2, 1)
        rs_copy(c, 3).start()
        rs_copy(c, 1).wait_recv()
        add(yx, 0)

    def rs3(c):
        lo, n = rchunks[c]
        cols = pl.ds(lo, n)
        rs_copy(c, 3).wait_recv()
        for zz in range(Z):
            G[t, zz, yx, :, cols] = (
                G[t, zz, yx, :, cols].astype(F32) + R2[zz, :, cols].astype(F32)
            ).astype(BF)
        for kind in (4, 5, 6):
            rs_copy(c, kind).start()

    def rs4(c):
        lo, n = rchunks[c]
        cols = pl.ds(lo, n)
        total = G[t, z, yx, :, cols].astype(F32)
        for kind in (4, 5, 6):
            rs_copy(c, kind).wait_recv()
            total = total + R3[kind - 4, :, cols].astype(F32)
        gpack[:, cols] = total * s.factor

    rs_steps = {"0": rs0, "1": rs1, "2": rs2, "3": rs3, "4": rs4}

    def weight_grad(lhs, rhs, c_lo, width, step):
        per = width // step

        def one(i, _):
            half = i // per
            lo = pl.multiple_of((i % per) * step, 128)
            y = nn(lhs[...], rhs[half, :, pl.ds(lo, step)]).astype(BF)
            G[half, :, :, :, pl.ds(pl.multiple_of(c_lo + lo, 128), step)] = y.reshape(Z, YX, D // GROUPS, step)
            return 0

        lax.fori_loop(0, 2 * per, one, 0)

    weight_grad(COTT, HID, C_DN, F2, 512)
    rs0(0)
    weight_grad(H2T, GI, C_UP, F2, 512)
    rs0(1)
    rs1(0)

    GP = HID

    weight_grad(GBT, O, C_OUT, H2W, H2W)
    rs0(2)
    rs1(1)

    def attend_back(i, _):
        b, half = i // 2, i % 2
        r = rows_of(b)
        do = nn(GB[r, :], wl(half, C_OUT, H2W)).astype(BF)
        q = QKV[half, r, 0:H2W]
        dpf = nt(VB[half], do)
        pf_low = PF[half, b]
        pf_all = pf_low.astype(F32)
        far_parts = []
        for pr in range(2):
            lanes = slice(pr * 128, (pr + 1) * 128)
            q2 = q[:, lanes]
            do2 = do[:, lanes]
            k2 = QKV[half, r, H2W + pr * 128:H2W + (pr + 1) * 128]
            v2 = QKV[half, r, 2 * H2W + pr * 128:2 * H2W + (pr + 1) * 128]
            dqs, dks, dvs = [], [], []
            for e in range(2):
                hl = 2 * pr + e
                dp = nt(v2, head_only(do2, e))
                p_low = PT[half, b, hl]
                p = p_low.astype(F32)
                df = dpf[16 * hl:16 * hl + 16]
                pf = pf_all[16 * hl:16 * hl + 16]
                corr = jnp.sum(p * dp, axis=0, keepdims=True) + jnp.sum(pf * df, axis=0, keepdims=True)
                ds = (p * (dp - corr)).astype(BF)
                far_parts.append(pf * (df - corr))
                dqs.append(tn(ds, k2))
                dks.append(nn(ds, q2))
                dvs.append(nn(p_low, do2))
            GP[half, r, H2W + pr * 128:H2W + (pr + 1) * 128] = jnp.where(even, dks[0], dks[1]).astype(BF)
            GP[half, r, 2 * H2W + pr * 128:2 * H2W + (pr + 1) * 128] = jnp.where(even, dvs[0], dvs[1]).astype(BF)
            MQ = jnp.where(even, dqs[0], dqs[1])
            if pr == 0:
                dq0 = MQ
            else:
                dq = jnp.concatenate([dq0, MQ], axis=1)
        dsf = jnp.concatenate(far_parts, axis=0).astype(BF)
        dq = (dq + tn(dsf, KB[half])) * (1.0 / math.sqrt(HD))
        GP[half, r, 0:H2W] = dq.astype(BF)
        DKS[half] += nn(dsf, q)
        DVS[half] += nn(pf_low, do)
        for when, todo in s.bwd_slots:
            @pl.when(i == when)
            def _():
                for name, c in todo:
                    rs_steps[name](c)
        return 0

    lax.fori_loop(0, 2 * NB, attend_back, 0)

    for half in range(2):
        for kind, src in ((0, DKS), (1, DVS)):
            kept = jnp.where(diagonal, src[half], 0.0)
            folded = kept[0:16] + kept[16:32] + kept[32:48] + kept[48:64]
            lo = (2 * half + kind) * H2W
            DSV[:, :, lo:lo + H2W] = folded.reshape(2, 8, H2W)
    dsv_copy = small_copy(2, DSV.at[1 - t], DSVR, pair)
    dsv_copy.start()
    dsv_copy.wait_recv()
    SHARE[...] = (DSV[t] + DSVR[...]) / own_counts

    for name, c in s.mid_slots:
        rs_steps[name](c)

    span_lane = iota((BLK, 128), 1)

    def last(b, _):
        r = rows_of(b)
        column = jnp.sum(jnp.where(span_lane == t * NB + b, SPC[...], 0.0), axis=1, keepdims=True)
        grad = None
        for half in range(2):
            lanes = slice(half * 2 * H2W, (half + 1) * 2 * H2W)
            shared = jnp.where(column == 0.0, SHARE[pl.ds(b, 1), lanes], SHARE[pl.ds(NB + b, 1), lanes])
            GP[half, r, H2W:QW] = (GP[half, r, H2W:QW].astype(F32) + shared).astype(BF)
            part = nt(GP[half, r, 0:QW], wl(half, 0, QW))
            grad = part if grad is None else grad + part
        unit, inverse = unit_rows(tok[r, :].astype(F32))
        e = grad * gain1[...]
        m1 = jnp.mean(e, axis=-1, keepdims=True)
        m2 = jnp.mean(e * unit, axis=-1, keepdims=True)
        dtok[r, :] = (MID[r, :] + inverse * (e - m1 - unit * m2)).astype(BF)
        ACC[0] += eight(grad * unit)
        return 0

    lax.fori_loop(0, NB, last, 0)

    weight_grad(H1T, GP, 0, QW, 384)
    rs0(3)

    folded = [jnp.sum(ACC[j], axis=0, keepdims=True) for j in range(4)]
    for half in range(2):
        line = jnp.sum(BUACC[half], axis=0, keepdims=True)
        folded += [line[:, j * D:(j + 1) * D] for j in range(F2 // D)]
    SM[0] = jnp.concatenate(folded, axis=0)

    def exchange(i, who):
        cp = small_copy(3 + i, SM.at[i], SMR.at[i], who)
        cp.start()
        cp.wait_recv()
        return SM[i] + SMR[i]

    SM[1] = exchange(0, pair)
    rs1(3)
    SM[2] = exchange(1, peer3)
    rs2(3)
    total = exchange(2, peer2)
    rs3(3)
    SM[3] = total
    for k in range(1, Z):
        small_copy(5 + k, SM.at[3], SMR.at[3 + (z + 0) % Z], zpeers[k - 1]).start()
    SMR[3 + z] = total
    for k in range(1, Z):
        small_copy(5 + k, SM.at[3], SMR.at[3 + (z + Z - k) % Z], zpeers[k - 1]).wait_recv()
    summed = (SMR[3] + SMR[4] + SMR[5] + SMR[6]) * s.factor
    o_gain1[...] = summed[0:1]
    o_gain2[...] = summed[1:2]
    o_bout[...] = summed[2:3]
    o_bdown[...] = summed[3:4]
    for j in range(2 * F2 // D):
        o_bup[:, j * D:(j + 1) * D] = summed[4 + j:5 + j]

    for name, c in s.end_slots:
        rs_steps[name](c)

    for c in range(len(chunks)):
        for kind in range(10):
            ag_copy(c, kind).wait_send()
    for c in range(len(rchunks)):
        for kind in range(7):
            rs_copy(c, kind).wait_send()
    bup_copy.wait_send()
    ksv_copy.wait_send()
    dsv_copy.wait_send()
    for i, who in enumerate((pair, peer3, peer2)):
        small_copy(3 + i, SM.at[i], SMR.at[i], who).wait_send()
    for k in range(1, Z):
        small_copy(5 + k, SM.at[3], SMR.at[3 + z], zpeers[k - 1]).wait_send()


def shards(
    tokens, cotangent, span_ids, gain_one, w_qkv, w_out, b_out, gain_two, w_up, b_up, w_down, b_down
):
    s = Sizes()
    dp = lax.axis_size("dp")
    s.sub = dp // GROUPS
    s.D = tokens.shape[2]
    s.rows = tokens.shape[1]
    s.NB = s.rows // BLK
    s.H2W = w_qkv.shape[2]
    s.F2 = w_up.shape[1]
    s.factor = 1.0 / math.sqrt(dp * lax.axis_size("tensor") * s.rows)
    sub, D, H2W, F2, N, NB = s.sub, s.D, s.H2W, s.F2, s.rows, s.NB
    QW = 3 * H2W
    width = QW + H2W + 2 * F2
    s.ag_chunks = [(0, 768), (768, 768), (1536, 768), (2304, 768)]
    s.rs_chunks = [(QW + H2W + F2, F2), (QW + H2W, F2), (QW, H2W), (0, QW)]
    s.fwd_slots = [(0, [("1", 2)]), (1, [("2", 2)]), (2, [("4", 1)]), (3, [("1", 3)]), (4, [("3", 2)]), (5, [("2", 3)])]
    s.tail_slots = [("4", 2), ("3", 3), ("4", 3)]
    s.bwd_slots = [(0, [("2", 0)]), (1, [("1", 2)]), (2, [("2", 1)]), (3, [("3", 0)]), (4, [("2", 2)]), (5, [("3", 1)]), (6, [("4", 0)]), (7, [("3", 2)])]
    s.mid_slots = [("4", 1), ("4", 2)]
    s.end_slots = [("4", 3)]
    pack = jnp.concatenate(
        [w_qkv.reshape(w_qkv.shape[0], QW), w_out.T, w_up, w_down.T], axis=1
    )
    groups = [[a * sub + b for b in range(sub)] for a in range(dp // sub)]
    if sub > 1:
        pack = lax.all_gather(pack, "dp", axis=0, tiled=True, axis_index_groups=groups)
    R = D // GROUPS

    def vm(*shape, dtype=BF):
        return pltpu.VMEM(shape, dtype)

    out = pl.pallas_call(
        functools.partial(kernel, s),
        out_shape=(
            jax.ShapeDtypeStruct((N, D), BF),
            jax.ShapeDtypeStruct((N, D), BF),
            jax.ShapeDtypeStruct((R, width), F32),
            jax.ShapeDtypeStruct((1, D), F32),
            jax.ShapeDtypeStruct((1, D), F32),
            jax.ShapeDtypeStruct((1, D), F32),
            jax.ShapeDtypeStruct((1, D), F32),
            jax.ShapeDtypeStruct((1, 2 * F2), F32),
        ),
        in_specs=[pl.BlockSpec(memory_space=pltpu.VMEM)] * 9,
        out_specs=[pl.BlockSpec(memory_space=pltpu.VMEM)] * 8,
        scratch_shapes=[
            vm(2, Z, YX, R, width),
            vm(2, Z, YX, R, width),
            vm(Z, YX, R, width),
            vm(2, Z, R, width),
            vm(Z, R, width),
            vm(Z - 1, R, width),
            vm(N, D),
            vm(D, N),
            vm(2, N, QW),
            vm(2, NB, 4, BLK, BLK),
            vm(2, NB, 64, BLK),
            vm(2, N, H2W),
            vm(N, D, dtype=F32),
            vm(N, D),
            vm(D, N),
            vm(D, N),
            vm(2, N, F2),
            vm(2, N, F2),
            vm(N, D),
            vm(D, N),
            vm(2, 8, F2, dtype=F32),
            vm(2, 8, 4 * H2W, dtype=F32),
            vm(2, 64, H2W),
            vm(2, 64, H2W),
            vm(2, 64, H2W, dtype=F32),
            vm(2, 64, H2W, dtype=F32),
            vm(2, 8, 4 * H2W, dtype=F32),
            vm(8, 4 * H2W, dtype=F32),
            vm(8, 4 * H2W, dtype=F32),
            vm(BLK, 128, dtype=F32),
            vm(8, N, dtype=F32),
            vm(2, 8, F2, dtype=F32),
            vm(4, 8, D, dtype=F32),
            vm(4, 8, D, dtype=F32),
            vm(7, 8, D, dtype=F32),
            pltpu.SemaphoreType.DMA((len(s.ag_chunks), 10)),
            pltpu.SemaphoreType.DMA((len(s.ag_chunks), 10)),
            pltpu.SemaphoreType.DMA((len(s.rs_chunks), 7)),
            pltpu.SemaphoreType.DMA((len(s.rs_chunks), 7)),
            pltpu.SemaphoreType.DMA((9,)),
            pltpu.SemaphoreType.DMA((9,)),
        ],
        compiler_params=pltpu.CompilerParams(
            collective_id=0, has_side_effects=True, vmem_limit_bytes=62 << 20
        ),
    )(
        tokens[0], cotangent[0], span_ids[0], gain_one[None], gain_two[None], b_out[None], b_down[None],
        b_up[None], pack,
    )
    result, d_tokens, grads, g1, g2, bo, bd, bu = out
    small = [g1[0], bo[0], g2[0], bu[0], bd[0]]
    if sub > 1:
        grads = lax.psum_scatter(grads, "dp", scatter_dimension=0, tiled=True, axis_index_groups=groups)
        small = [v for v in lax.psum(tuple(small), "dp", axis_index_groups=groups)]
    n = grads.shape[0]
    return (
        result[None],
        d_tokens[None],
        small[0],
        grads[:, :QW].reshape(n, 3, H2W),
        grads[:, QW:QW + H2W].T,
        small[1],
        small[2],
        grads[:, QW + H2W:QW + H2W + F2],
        small[3],
        grads[:, QW + H2W + F2:].T,
        small[4],
    )


def solution(mesh):
    in_specs = (
        P("dp", "tensor", None),
        P("dp", "tensor", None),
        P("dp", None, None),
        P(),
        P("dp", None, "tensor"),
        P("tensor", "dp"),
        P(),
        P(),
        P("dp", "tensor"),
        P("tensor"),
        P("tensor", "dp"),
        P(),
    )
    out_specs = (
        P("dp", "tensor", None),
        P("dp", "tensor", None),
        P(),
        P("dp", None, "tensor"),
        P("tensor", "dp"),
        P(),
        P(),
        P("dp", "tensor"),
        P(),
        P("tensor", "dp"),
        P(),
    )
    return jax.shard_map(shards, mesh=mesh, in_specs=in_specs, out_specs=out_specs, check_vma=False)
```

```python
import functools
import math

import jax
import jax.numpy as jnp
from jax import lax
from jax.experimental import pallas as pl
from jax.experimental.pallas import tpu as pltpu
from jax.sharding import PartitionSpec as P

HD = 64
BLK = 256
EPS = 1e-05
MASKED = -1e30
Z = 4
YX = 4
GROUPS = Z * YX
F32 = jnp.float32
BF = jnp.bfloat16
MESH = pl.DeviceIdType.MESH


def dot(a, b, ca, cb):
    return lax.dot_general(a, b, (((ca,), (cb,)), ((), ())), preferred_element_type=F32)


def nn(a, b):
    return dot(a, b, 1, 0)


def nt(a, b):
    return dot(a, b, 1, 1)


def tn(a, b):
    return dot(a, b, 0, 0)


def iota(shape, axis):
    return lax.broadcasted_iota(jnp.int32, shape, axis)


def unit_rows(values):
    centre = values - jnp.mean(values, axis=-1, keepdims=True)
    spread = jnp.mean(centre * centre, axis=-1, keepdims=True)
    inverse = lax.rsqrt(spread + EPS)
    return centre * inverse, inverse


def eight(values):
    return jnp.sum(values.reshape(values.shape[0] // 8, 8, values.shape[1]), axis=0)


class Sizes:
    pass


def kernel(s, *refs):
    (tok_in, cot_in, span, gain1, gain2, bout, bdown, bup_own, s_qkv, s_out, s_up, s_dn) = refs[:12]
    (res_out, dtok_out, g_qkv, g_out, g_up, g_dn, o_gain1, o_gain2, o_bout, o_bdown, o_bup) = refs[12:23]
    (W, G, R0, R1, R2, R3, H1, H1T, QKV, PT, PF, O, MID, H2, H2T, COTT, HID, GI, GB, GBT,
     BUP, KSV, KB, VB, DKS, DVS, DSV, DSVR, SHARE, SPC, M8, BUACC, ACC, SM, SMR, tok, cot, RES, GO,
     ag_s, ag_r, rs_s, rs_r, sx_s, sx_r, lc, oc) = refs[23:]
    D, H2W, F2, NB = s.D, s.H2W, s.F2, s.NB
    QW = 3 * H2W
    FC, NFC = s.FC, F2 // s.FC
    C_OUT = QW

    def c_up(fc):
        return QW + H2W + 2 * FC * fc

    def c_dn(fc):
        return QW + H2W + 2 * FC * fc + FC

    d = lax.axis_index("dp")
    t = lax.axis_index("tensor")
    g = d // s.sub
    z = g // YX
    yx = g % YX
    rest = d % s.sub
    b2 = 2 - t
    b3 = 1 + t

    def at(zz, q):
        return ((zz * YX + q) * s.sub + rest, t)

    def flip(q, bit):
        y_bit, x_bit = q // 2, q % 2
        return jnp.where(bit == 2, (1 - y_bit) * 2 + x_bit, y_bit * 2 + 1 - x_bit)

    yx2 = flip(yx, b2)
    yx3 = flip(yx, b3)
    yx23 = 3 - yx
    pair = (d, 1 - t)
    peer2 = at(z, yx2)
    peer3 = at(z, yx3)
    zpeers = [at((z + k) % Z, yx) for k in range(1, Z)]

    barrier = pltpu.get_barrier_semaphore()
    for who in [pair, peer2, peer3] + zpeers:
        pl.semaphore_signal(barrier, inc=1, device_id=who, device_id_type=MESH)

    fetches = []

    def fetch(src, dst):
        cp = pltpu.make_async_copy(src, dst, lc.at[len(fetches)])
        cp.start()
        fetches.append(cp)

    own = W.at[t, z, yx]
    for j in range(3):
        for pr in range(2):
            fetch(s_qkv.at[j, :, pl.ds(128 * pr, 128)], own.at[:, pl.ds(384 * pr + 128 * j, 128)])
    fetch(s_out, own.at[:, pl.ds(C_OUT, H2W)])
    for fc in range(NFC):
        fetch(s_up.at[:, pl.ds(fc * FC, FC)], own.at[:, pl.ds(c_up(fc), FC)])
        fetch(s_dn.at[:, pl.ds(fc * FC, FC)], own.at[:, pl.ds(c_dn(fc), FC)])
    n_shards = len(fetches)
    fetch(tok_in, tok)
    fetch(cot_in, cot)
    BUP[t] = jnp.broadcast_to(bup_own[...], (8, F2))

    half_rows = iota((8, BLK), 0)
    for b in range(NB):
        line = span[pl.ds(t * NB + b, 1), :]
        belongs = jnp.logical_and(half_rows // NB == line, half_rows % NB == b)
        M8[:, b * BLK:(b + 1) * BLK] = belongs.astype(F32)
    SPC[...] = jnp.concatenate([span[...].astype(F32), jnp.zeros((120, BLK), F32)], axis=0).T
    zeros_in = (span[...] == 0).astype(F32)
    ones_in = (span[...] == 1).astype(F32)
    n_zero = jnp.sum(zeros_in, axis=1, keepdims=True)
    n_one = jnp.sum(ones_in, axis=1, keepdims=True)
    counts = jnp.concatenate(
        [n_zero[:NB], n_one[:NB], n_zero[NB:2 * NB], n_one[NB:2 * NB]], axis=0
    )
    log_counts = jnp.concatenate([jnp.log(counts)] * 4, axis=0)
    own_counts = jnp.sum(M8[...], axis=1, keepdims=True)
    code = iota((64, 1), 0) % 16
    block_of = (code // 8) * NB + code % NB

    for cp in fetches[:n_shards]:
        cp.wait()
    pl.semaphore_wait(barrier, 3 + Z - 1)

    def remote(src, dst, ss, rs, who):
        return pltpu.make_async_remote_copy(
            src_ref=src, dst_ref=dst, send_sem=ss, recv_sem=rs, device_id=who, device_id_type=MESH
        )

    chunks = s.ag_chunks
    group_of = {"o": yx, "2": yx2, "3": yx3, "23": yx23}
    kinds = ["z1", "z2", "z3"] + [a + str(k) for a in ("2s", "3s", "3t") for k in range(Z)]
    kinds += ["p" + a + "_" + str(k) for a in group_of for k in range(Z)]
    number = {kind: i for i, kind in enumerate(kinds)}

    def ag_copy(c, kind, got=False):
        lo, n = chunks[c]
        cols = pl.ds(lo, n)
        if kind[0] == "z":
            k = int(kind[1])
            window, who = W.at[t, (z + Z - k) % Z if got else z, yx, :, cols], zpeers[k - 1]
        elif kind[0] == "p":
            name, k = kind[1:].split("_")
            window, who = W.at[1 - t if got else t, (z + Z - int(k)) % Z, group_of[name], :, cols], pair
        else:
            there, here, who = {"2s": (yx2, yx, peer2), "3s": (yx3, yx, peer3), "3t": (yx23, yx2, peer3)}[kind[:2]]
            window = W.at[t, (z + Z - int(kind[2])) % Z, there if got else here, :, cols]
        i = number[kind]
        return remote(window, window, ag_s.at[c, i], ag_r.at[c, i], who)

    def ag_event(event):
        c, got, starts = event
        if got is not None:
            ag_copy(c, got, True).wait_recv()
        for kind in starts:
            ag_copy(c, kind).start()

    def ag_done(c):
        for name in group_of:
            for k in range(Z):
                ag_copy(c, "p" + name + "_" + str(k), True).wait_recv()

    order = (1, 3, 2)
    after = (0, 1, 3, 2)

    def ag_events(c):
        first = [(c, None, ["z1", "z3", "z2", "2s0", "3s0", "po_0"])]
        second = [(c, f"z{k}", [f"2s{k}", f"3s{k}", f"po_{k}"]) for k in order]
        third = [(c, f"2s{k}", [f"3t{k}", f"p2_{k}"]) for k in after]
        fourth = [(c, f"3s{k}", [f"p3_{k}"]) for k in after]
        fifth = [(c, f"3t{k}", [f"p23_{k}"]) for k in after]
        return [first, second, third, fourth, fifth]

    gathers = [sum(ag_events(c), []) for c in range(len(chunks))]

    def run(events):
        for kind, c, step in events:
            if kind == "a":
                ag_event(gathers[c][step])
            elif kind == "r":
                rs_steps[step](c)
            else:
                small_step(step)

    def in_slots(i, places):
        for when, events in enumerate(places):
            if events:
                @pl.when(i == when)
                def _():
                    run(events)

    def small_copy(i, src, dst, who):
        return remote(src, dst, sx_s.at[i], sx_r.at[i], who)

    def exchange(i, who):
        return small_copy(4 + i, SM.at[i], SMR.at[i], who)

    def small_step(i):
        whos = (pair, peer3, peer2)
        if i > 0:
            exchange(i - 1, whos[i - 1]).wait_recv()
            SM[i] = SM[i - 1] + SMR[i - 1]
        if i < 3:
            exchange(i, whos[i]).start()
        else:
            SMR[3 + z] = SM[3]
            for k in range(1, Z):
                small_copy(6 + k, SM.at[3], SMR.at[3 + z], zpeers[k - 1]).start()

    run(s.plan["first"])
    bup_copy = small_copy(0, BUP.at[t], BUP.at[t], pair)
    bup_copy.start()

    def wl(half, lo, n):
        return W[half, :, :, :, pl.ds(lo, n)].reshape(D, n)

    def rows_of(b):
        return pl.ds(pl.multiple_of(b * BLK, BLK), BLK)

    for cp in fetches[n_shards:]:
        cp.wait()

    def norm_one(b, _):
        r = rows_of(b)
        unit, _inv = unit_rows(tok[r, :].astype(F32))
        low = (unit * gain1[...]).astype(BF)
        H1[r, :] = low
        H1T[:, r] = low.T
        COTT[:, r] = cot[r, :].T
        return 0

    lax.fori_loop(0, NB, norm_one, 0)

    BUACC[...] = jnp.zeros_like(BUACC)
    ACC[...] = jnp.zeros_like(ACC)
    DKS[...] = jnp.zeros_like(DKS)
    DVS[...] = jnp.zeros_like(DVS)

    run(s.plan["second"])
    ag_done(0)

    q_scale = jnp.where(iota((1, QW), 1) % 384 < 128, 1.0 / math.sqrt(HD), 1.0).astype(F32)

    def project(i, _):
        b, half = i // 2, i % 2
        r = rows_of(b)
        y = nn(H1[r, :], wl(half, 0, QW)) * q_scale
        QKV[half, r, :] = y.astype(BF)
        in_slots(i, s.plan["project"])
        return 0

    lax.fori_loop(0, 2 * NB, project, 0)

    member_low = jnp.concatenate([M8[...], M8[...]], axis=0).astype(BF)
    for half in range(2):
        for pr in range(2):
            sums = nn(member_low, QKV[half, :, 384 * pr + 128:384 * pr + 384])[:8]
            means = (sums / own_counts).astype(BF).astype(F32)
            for kind in range(2):
                lo = (2 * half + kind) * H2W + 128 * pr
                KSV[t, :, lo:lo + 128] = means[:, 128 * kind:128 * kind + 128]
    ksv_copy = small_copy(1, KSV.at[t], KSV.at[t], pair)
    ksv_copy.start()
    run(s.plan["third"])
    small_copy(1, KSV.at[1 - t], KSV.at[1 - t], pair).wait_recv()
    diagonal = iota((64, H2W), 0) // 16 == iota((64, H2W), 1) // HD
    everything = KSV[...].reshape(16, 4 * H2W)
    for half in range(2):
        for kind, out in ((0, KB), (1, VB)):
            lo = (2 * half + kind) * H2W
            tiled = jnp.concatenate([everything[:, lo:lo + H2W]] * 4, axis=0)
            out[half] = jnp.where(diagonal, tiled, 0.0).astype(BF)

    even = iota((BLK, 128), 1) < HD

    def head_only(values, e):
        return jnp.where(even if e == 0 else jnp.logical_not(even), values, jnp.zeros_like(values))

    def attend(i, _):
        b, half = i // 2, i % 2
        r = rows_of(b)
        q = jnp.concatenate([QKV[half, r, 0:128], QKV[half, r, 384:512]], axis=1)
        far = nt(KB[half], q) + log_counts
        far = jnp.where(block_of < t * NB + b, far, MASKED)
        parts, far_parts = [], []
        for pr in range(2):
            lanes = slice(pr * 128, (pr + 1) * 128)
            q2 = q[:, lanes]
            k2 = QKV[half, r, pr * 384 + 128:pr * 384 + 256]
            v2 = QKV[half, r, pr * 384 + 256:pr * 384 + 384]
            both = []
            for e in range(2):
                hl = 2 * pr + e
                near = nt(k2, head_only(q2, e))
                sf = far[16 * hl:16 * hl + 16]
                largest = jnp.maximum(
                    jnp.max(near, axis=0, keepdims=True), jnp.max(sf, axis=0, keepdims=True)
                )
                pn = jnp.exp(near - largest)
                pf = jnp.exp(sf - largest)
                total = jnp.sum(pn, axis=0, keepdims=True) + jnp.sum(pf, axis=0, keepdims=True)
                inv = 1.0 / total
                pn = (pn * inv).astype(BF)
                PT[half, b, hl] = pn
                far_parts.append(pf * inv)
                both.append(tn(pn, v2))
            parts.append(jnp.where(even, both[0], both[1]))
        pf_all = jnp.concatenate(far_parts, axis=0).astype(BF)
        PF[half, b] = pf_all
        out = jnp.concatenate(parts, axis=1) + tn(pf_all, VB[half])
        O[half, r, :] = out.astype(BF)
        in_slots(i, s.plan["attend"])
        return 0

    lax.fori_loop(0, 2 * NB, attend, 0)

    run(s.plan["proj_wait"])
    ag_done(1)
    small_copy(0, BUP.at[1 - t], BUP.at[1 - t], pair).wait_recv()

    def out_proj(b, _):
        r = rows_of(b)
        branch = nt(O[0, r, :], wl(0, C_OUT, H2W)) + nt(O[1, r, :], wl(1, C_OUT, H2W))
        middle = tok[r, :].astype(F32) + (branch + bout[...])
        MID[r, :] = middle
        unit, _inv = unit_rows(middle)
        low = (unit * gain2[...]).astype(BF)
        H2[r, :] = low
        H2T[:, r] = low.T
        in_slots(b, s.plan["proj"])
        return 0

    lax.fori_loop(0, NB, out_proj, 0)

    c0 = math.sqrt(2.0 / math.pi)
    c1 = c0 * 0.044715

    def feed(fc):
        def one(i, _):
            b, half = i // 2, i % 2
            r = rows_of(b)
            cols = slice(fc * FC, (fc + 1) * FC)
            x = nn(H2[r, :], wl(half, c_up(fc), FC)) + BUP[half, 0:1, cols]
            gh = nn(cot[r, :], wl(half, c_dn(fc), FC))
            sq = x * x
            th = jnp.tanh(x * (c0 + c1 * sq))
            up = 0.5 + 0.5 * th
            HID[half, r, cols] = (x * up).astype(BF)
            slope = up + (0.5 * x) * (1.0 - th * th) * (c0 + (3.0 * c1) * sq)
            gi = gh * slope
            GI[half, r, cols] = gi.astype(BF)
            BUACC[half, :, cols] += eight(gi)
            in_slots(i, s.plan["feed" + str(fc)])
            return 0

        lax.fori_loop(0, 2 * NB, one, 0)

    def over_units(values, r, place):
        total = None
        for half in range(2):
            for fc in range(NFC):
                part = nt(values[half, r, fc * FC:(fc + 1) * FC], wl(half, place(fc), FC))
                total = part if total is None else total + part
        return total

    def feed_back(b, _):
        r = rows_of(b)
        middle = MID[r, :]
        RES[r, :] = middle
        g2 = over_units(GI, r, c_up)
        unit, inverse = unit_rows(middle)
        e = g2 * gain2[...]
        m1 = jnp.mean(e, axis=-1, keepdims=True)
        m2 = jnp.mean(e * unit, axis=-1, keepdims=True)
        grad_out = cot[r, :].astype(F32)
        mid = grad_out + inverse * (e - m1 - unit * m2)
        MID[r, :] = mid
        low = mid.astype(BF)
        GB[r, :] = low
        GBT[:, r] = low.T
        for half in range(2):
            GO[half, r, :] = nn(low, wl(half, C_OUT, H2W)).astype(BF)
        ACC[1] += eight(g2 * unit)
        ACC[2] += eight(mid)
        ACC[3] += eight(grad_out)
        in_slots(b, s.plan["feed_back"])
        return 0

    def give(b, _):
        r = rows_of(b)
        H1[r, :] = (RES[r, :] + (over_units(HID, r, c_dn) + bdown[...])).astype(BF)
        in_slots(b, s.plan["give"])
        return 0

    rchunks = s.rs_chunks

    def rs_copy(c, kind):
        lo, n = rchunks[c]
        cols = pl.ds(lo, n)
        if kind == 0:
            src, dst, who = G.at[1 - t, :, :, :, cols], R0.at[:, :, :, cols], pair
        elif kind == 1:
            src, dst, who = G.at[t, :, yx3, :, cols], R1.at[0, :, :, cols], peer3
        elif kind == 2:
            src, dst, who = G.at[t, :, yx23, :, cols], R1.at[1, :, :, cols], peer3
        elif kind == 3:
            src, dst, who = G.at[t, :, yx2, :, cols], R2.at[:, :, cols], peer2
        else:
            k = kind - 3
            src, dst, who = G.at[t, (z + k) % Z, yx, :, cols], R3.at[k - 1, :, cols], zpeers[k - 1]
        return remote(src, dst, rs_s.at[c, kind], rs_r.at[c, kind], who)

    def rs0(c):
        rs_copy(c, 0).start()

    def rs1(c):
        lo, n = rchunks[c]
        rs_copy(c, 0).wait_recv()
        cols = pl.ds(lo, n)

        def add(q):
            for zz in range(Z):
                G[t, zz, q, :, cols] = (
                    G[t, zz, q, :, cols].astype(F32) + R0[zz, q, :, cols].astype(F32)
                ).astype(BF)

        add(yx23)
        rs_copy(c, 2).start()
        add(yx3)
        rs_copy(c, 1).start()
        add(yx2)
        add(yx)

    def rs2(c):
        lo, n = rchunks[c]
        cols = pl.ds(lo, n)

        def add(q, j):
            for zz in range(Z):
                G[t, zz, q, :, cols] = (
                    G[t, zz, q, :, cols].astype(F32) + R1[j, zz, :, cols].astype(F32)
                ).astype(BF)

        rs_copy(c, 2).wait_recv()
        add(yx2, 1)
        rs_copy(c, 3).start()
        rs_copy(c, 1).wait_recv()
        add(yx, 0)

    def rs3(c):
        lo, n = rchunks[c]
        cols = pl.ds(lo, n)
        rs_copy(c, 3).wait_recv()
        for zz in range(Z):
            G[t, zz, yx, :, cols] = (
                G[t, zz, yx, :, cols].astype(F32) + R2[zz, :, cols].astype(F32)
            ).astype(BF)
        for kind in (4, 5, 6):
            rs_copy(c, kind).start()

    def rs4(c):
        lo, n = rchunks[c]
        cols = pl.ds(lo, n)
        total = G[t, z, yx, :, cols].astype(F32)
        for kind in (4, 5, 6):
            rs_copy(c, kind).wait_recv()
            total = total + R3[kind - 4, :, cols].astype(F32)
        total = total * s.factor
        if lo < QW:
            for j in range(3):
                g_qkv[j, :, lo // 3:lo // 3 + 128] = total[:, 128 * j:128 * j + 128]
        elif lo == C_OUT:
            g_out[...] = total
        else:
            for part in range(n // FC):
                place = (lo - QW - H2W) // FC + part
                dst = g_dn if place % 2 else g_up
                dst[:, (place // 2) * FC:(place // 2 + 1) * FC] = total[:, part * FC:(part + 1) * FC]

    rs_steps = (rs0, rs1, rs2, rs3, rs4)

    def weight_grad(lhs, rhs, lo, c_lo, n):
        def one(half, _):
            y = nn(lhs[...], rhs[half, :, pl.ds(lo, n)]).astype(BF)
            G[half, :, :, :, pl.ds(c_lo, n)] = y.reshape(Z, YX, D // GROUPS, n)
            return 0

        lax.fori_loop(0, 2, one, 0)

    for fc in range(NFC):
        if fc == NFC - 1:
            run(s.plan["feed1_wait"])
            ag_done(2)
        feed(fc)
        weight_grad(H2T, GI, fc * FC, c_up(fc), FC)
        run(s.plan["w" + str(2 * fc)])
        weight_grad(COTT, HID, fc * FC, c_dn(fc), FC)
        run(s.plan["w" + str(2 * fc + 1)])

    lax.fori_loop(0, NB, feed_back, 0)
    weight_grad(GBT, O, 0, C_OUT, H2W)
    run(s.plan["out"])

    GP = GI
    halves = iota((32, 128), 0) // 16 == iota((32, 128), 1) // HD

    def attend_back(pr):
        lo = 384 * pr

        def one(i, _):
            b, half = i // 2, i % 2
            r = rows_of(b)
            q2 = QKV[half, r, lo:lo + 128]
            k2 = QKV[half, r, lo + 128:lo + 256]
            v2 = QKV[half, r, lo + 256:lo + 384]
            do2 = GO[half, r, 128 * pr:128 * pr + 128]
            means_k = KB[half, 32 * pr:32 * pr + 32, 128 * pr:128 * pr + 128]
            means_v = VB[half, 32 * pr:32 * pr + 32, 128 * pr:128 * pr + 128]
            pf_low = PF[half, b, 32 * pr:32 * pr + 32]
            dpf = nt(means_v, do2)
            pf_all = pf_low.astype(F32)
            far_parts, dqs, dks, dvs = [], [], [], []
            for e in range(2):
                dp = nt(v2, head_only(do2, e))
                p_low = PT[half, b, 2 * pr + e]
                p = p_low.astype(F32)
                df = dpf[16 * e:16 * e + 16]
                pf = pf_all[16 * e:16 * e + 16]
                corr = jnp.sum(p * dp, axis=0, keepdims=True) + jnp.sum(pf * df, axis=0, keepdims=True)
                ds = (p * (dp - corr)).astype(BF)
                far_parts.append(pf * (df - corr))
                dqs.append(tn(ds, k2))
                dks.append(nn(ds, q2))
                dvs.append(nn(p_low, do2))
            dsf = jnp.concatenate(far_parts, axis=0).astype(BF)
            dq = (jnp.where(even, dqs[0], dqs[1]) + tn(dsf, means_k)) * (1.0 / math.sqrt(HD))
            GP[half, r, lo:lo + 128] = dq.astype(BF)
            GP[half, r, lo + 128:lo + 256] = jnp.where(even, dks[0], dks[1]).astype(BF)
            GP[half, r, lo + 256:lo + 384] = jnp.where(even, dvs[0], dvs[1]).astype(BF)
            DKS[half, pr] += nn(dsf, q2)
            DVS[half, pr] += nn(pf_low, do2)
            in_slots(i, s.plan["back" + str(pr)])
            return 0

        lax.fori_loop(0, 2 * NB, one, 0)

        for half in range(2):
            for kind, src in ((0, DKS), (1, DVS)):
                kept = jnp.where(halves, src[half, pr], 0.0)
                at_lane = (2 * half + kind) * 128
                DSV[pr, :, :, at_lane:at_lane + 128] = (kept[0:16] + kept[16:32]).reshape(2, 8, 128)
        small_copy(2 + pr, DSV.at[pr, 1 - t], DSVR.at[pr], pair).start()
        run(s.plan["share" + str(pr)])
        small_copy(2 + pr, DSV.at[pr, 1 - t], DSVR.at[pr], pair).wait_recv()
        SHARE[pr] = (DSV[pr, t] + DSVR[pr]) / own_counts

        def spread(b, _):
            r = rows_of(b)
            column = jnp.sum(jnp.where(span_lane == t * NB + b, SPC[...], 0.0), axis=1, keepdims=True)
            for half in range(2):
                lanes = slice(256 * half, 256 * half + 256)
                shared = jnp.where(
                    column == 0.0, SHARE[pr, pl.ds(b, 1), lanes], SHARE[pr, pl.ds(NB + b, 1), lanes]
                )
                GP[half, r, lo + 128:lo + 384] = (GP[half, r, lo + 128:lo + 384].astype(F32) + shared).astype(BF)
            return 0

        lax.fori_loop(0, NB, spread, 0)
        run(s.plan["spread" + str(pr)])
        weight_grad(H1T, GP, lo, lo, 384)
        run(s.plan["q" + str(pr)])

    span_lane = iota((BLK, 128), 1)
    attend_back(0)
    attend_back(1)

    def last(b, _):
        r = rows_of(b)
        grad = nt(GP[0, r, 0:QW], wl(0, 0, QW)) + nt(GP[1, r, 0:QW], wl(1, 0, QW))
        unit, inverse = unit_rows(tok[r, :].astype(F32))
        e = grad * gain1[...]
        m1 = jnp.mean(e, axis=-1, keepdims=True)
        m2 = jnp.mean(e * unit, axis=-1, keepdims=True)
        H2[r, :] = (MID[r, :] + inverse * (e - m1 - unit * m2)).astype(BF)
        ACC[0] += eight(grad * unit)
        in_slots(b, s.plan["last"])
        return 0

    lax.fori_loop(0, NB, last, 0)
    out_copies = [pltpu.make_async_copy(H2, dtok_out, oc.at[0]), pltpu.make_async_copy(H1, res_out, oc.at[1])]
    out_copies[0].start()

    folded = [jnp.sum(ACC[j], axis=0, keepdims=True) for j in range(4)]
    for half in range(2):
        line = jnp.sum(BUACC[half], axis=0, keepdims=True)
        folded += [line[:, j * D:(j + 1) * D] for j in range(F2 // D)]
    SM[0] = jnp.concatenate(folded, axis=0)

    run(s.plan["small"])
    lax.fori_loop(0, NB, give, 0)
    out_copies[1].start()
    run(s.plan["end"])
    for k in range(1, Z):
        small_copy(6 + k, SM.at[3], SMR.at[3 + (z + Z - k) % Z], zpeers[k - 1]).wait_recv()
    summed = (SMR[3] + SMR[4] + SMR[5] + SMR[6]) * s.factor
    o_gain1[...] = summed[0:1]
    o_gain2[...] = summed[1:2]
    o_bout[...] = summed[2:3]
    o_bdown[...] = summed[3:4]
    for j in range(2 * F2 // D):
        o_bup[:, j * D:(j + 1) * D] = summed[4 + j:5 + j]


    for cp in out_copies:
        cp.wait()
    for c in range(len(chunks)):
        for kind in kinds:
            ag_copy(c, kind).wait_send()
    for c in range(len(rchunks)):
        for kind in range(7):
            rs_copy(c, kind).wait_send()
    bup_copy.wait_send()
    ksv_copy.wait_send()
    for pr in range(2):
        small_copy(2 + pr, DSV.at[pr, 1 - t], DSVR.at[pr], pair).wait_send()
    for i, who in enumerate((pair, peer3, peer2)):
        exchange(i, who).wait_send()
    for k in range(1, Z):
        small_copy(6 + k, SM.at[3], SMR.at[3 + z], zpeers[k - 1]).wait_send()


def deliver(n, *refs):
    ins, outs, held, (got, sent) = refs[:n], refs[n:2 * n], refs[2 * n:3 * n], refs[3 * n:]
    firsts = [pltpu.make_async_copy(ins[i], held[i], got.at[i]) for i in range(n)]
    seconds = [pltpu.make_async_copy(held[i], outs[i], sent.at[i]) for i in range(n)]
    for cp in firsts:
        cp.start()
    for first, second in zip(firsts, seconds):
        first.wait()
        second.start()
    for cp in seconds:
        cp.wait()


def shards(
    tokens, cotangent, span_ids, gain_one, w_qkv, w_out, b_out, gain_two, w_up, b_up, w_down, b_down
):
    s = Sizes()
    dp = lax.axis_size("dp")
    s.sub = dp // GROUPS
    s.D = tokens.shape[2]
    s.rows = tokens.shape[1]
    s.NB = s.rows // BLK
    s.H2W = w_qkv.shape[2]
    s.F2 = w_up.shape[1]
    s.factor = 1.0 / math.sqrt(dp * lax.axis_size("tensor") * s.rows)
    sub, D, H2W, F2, N, NB = s.sub, s.D, s.H2W, s.F2, s.rows, s.NB
    QW = 3 * H2W
    width = QW + H2W + 2 * F2
    s.FC = 512
    s.FC = 512
    s.ag_chunks = [(0, 768), (768, 1280), (2048, 1024)]
    s.rs_chunks = [(1024, 512), (1536, 512), (2048, 512), (2560, 512), (768, 256), (0, 384), (384, 384)]
    s.plan = {
        "first": (('a', 0, 0), ),
        "second": (('a', 0, 4), ('a', 0, 8), ('a', 0, 1), ('a', 0, 12), ('a', 0, 2), ('a', 0, 5), ('a', 0, 9), ('a', 0, 3), ('a', 1, 0), ('a', 0, 6), ('a', 0, 10), ('a', 0, 13), ('a', 0, 7), ('a', 0, 11), ('a', 1, 4), ('a', 1, 8), ('a', 1, 1), ('a', 0, 14), ('a', 0, 15), ('a', 1, 2), ('a', 1, 12), ),
        "third": (('a', 1, 13), ),
        "proj_wait": (),
        "feed1_wait": (),
        "w0": (('r', 0, 0), ),
        "w1": (('r', 1, 0), ),
        "w2": (('r', 2, 0), ),
        "w3": (('r', 3, 0), ('r', 1, 2), ),
        "out": (('r', 4, 0), ('r', 2, 2), ),
        "share0": (),
        "spread0": (('r', 4, 3), ('r', 2, 4), ),
        "q0": (('r', 5, 0), ),
        "share1": (),
        "spread1": (('r', 5, 3), ),
        "q1": (('r', 6, 0), ),
        "small": (('s', 0, 0), ),
        "end": (('r', 6, 2), ('s', 0, 2), ('r', 6, 3), ('s', 0, 3), ('r', 6, 4), ),
        "project": (
            (),
            (('a', 1, 5), ),
            (),
            (('a', 1, 9), ),
            (),
            (('a', 1, 6), ),
            (),
            (('a', 1, 3), ('a', 2, 0), ('a', 1, 10), ),
        ),
        "attend": (
            (('a', 1, 14), ('a', 1, 7), ),
            (('a', 1, 11), ),
            (('a', 2, 1), ('a', 2, 4), ),
            (('a', 2, 8), ),
            (('a', 2, 2), ('a', 1, 15), ),
            (('a', 2, 5), ),
            (('a', 2, 9), ),
            (('a', 2, 12), ('a', 2, 3), ('a', 2, 6), ),
        ),
        "proj": (
            (('a', 2, 10), ),
            (('a', 2, 13), ),
            (),
            (('a', 2, 7), ),
        ),
        "feed0": (
            (('a', 2, 11), ),
            (('a', 2, 14), ),
            (),
            (('a', 2, 15), ),
            (),
            (),
            (),
            (),
        ),
        "feed1": (
            (('r', 0, 1), ),
            (),
            (('r', 1, 1), ),
            (),
            (),
            (),
            (),
            (('r', 0, 2), ),
        ),
        "feed_back": (
            (('r', 2, 1), ('r', 0, 3), ),
            (('r', 3, 1), ),
            (('r', 1, 3), ),
            (),
        ),
        "back0": (
            (('r', 0, 4), ),
            (('r', 4, 1), ),
            (('r', 3, 2), ),
            (('r', 1, 4), ('r', 2, 3), ),
            (),
            (('r', 4, 2), ),
            (('r', 3, 3), ),
            (),
        ),
        "back1": (
            (),
            (('r', 3, 4), ('r', 5, 1), ),
            (('r', 4, 4), ),
            (),
            (),
            (('r', 5, 2), ),
            (),
            (),
        ),
        "last": (
            (),
            (),
            (('r', 6, 1), ),
            (('r', 5, 4), ),
        ),
        "give": (
            (),
            (('s', 0, 1), ),
            (),
            (),
        ),
    }
    groups = [[a * sub + b for b in range(sub)] for a in range(dp // sub)]
    pieces = [jnp.transpose(w_qkv, (1, 0, 2)), w_out.T, w_up, w_down.T]
    if sub > 1:
        pieces = [
            lax.all_gather(piece, "dp", axis=piece.ndim - 2, tiled=True, axis_index_groups=groups)
            for piece in pieces
        ]
    R = D // GROUPS

    def vm(*shape, dtype=BF):
        return pltpu.VMEM(shape, dtype)

    any_space = pl.BlockSpec(memory_space=pl.ANY)
    in_vmem = pl.BlockSpec(memory_space=pltpu.VMEM)
    results = (
        jax.ShapeDtypeStruct((N, D), BF),
        jax.ShapeDtypeStruct((N, D), BF),
        jax.ShapeDtypeStruct((3, R, H2W), F32),
        jax.ShapeDtypeStruct((R, H2W), F32),
        jax.ShapeDtypeStruct((R, F2), F32),
        jax.ShapeDtypeStruct((R, F2), F32),
        jax.ShapeDtypeStruct((1, D), F32),
        jax.ShapeDtypeStruct((1, D), F32),
        jax.ShapeDtypeStruct((1, D), F32),
        jax.ShapeDtypeStruct((1, D), F32),
        jax.ShapeDtypeStruct((1, 2 * F2), F32),
    )
    out = pl.pallas_call(
        functools.partial(kernel, s),
        out_shape=results,
        in_specs=[any_space] * 2 + [in_vmem] * 6 + [any_space] * 4,
        out_specs=[any_space] * 2 + [in_vmem] * 9,
        scratch_shapes=[
            vm(2, Z, YX, R, width),
            vm(2, Z, YX, R, width),
            vm(Z, YX, R, width),
            vm(2, Z, R, width),
            vm(Z, R, width),
            vm(Z - 1, R, width),
            vm(N, D),
            vm(D, N),
            vm(2, N, QW),
            vm(2, NB, 4, BLK, BLK),
            vm(2, NB, 64, BLK),
            vm(2, N, H2W),
            vm(N, D, dtype=F32),
            vm(N, D),
            vm(D, N),
            vm(D, N),
            vm(2, N, F2),
            vm(2, N, F2),
            vm(N, D),
            vm(D, N),
            vm(2, 8, F2, dtype=F32),
            vm(2, 8, 4 * H2W, dtype=F32),
            vm(2, 64, H2W),
            vm(2, 64, H2W),
            vm(2, 2, 32, 128, dtype=F32),
            vm(2, 2, 32, 128, dtype=F32),
            vm(2, 2, 8, 512, dtype=F32),
            vm(2, 8, 512, dtype=F32),
            vm(2, 8, 512, dtype=F32),
            vm(BLK, 128, dtype=F32),
            vm(8, N, dtype=F32),
            vm(2, 8, F2, dtype=F32),
            vm(4, 8, D, dtype=F32),
            vm(4, 8, D, dtype=F32),
            vm(7, 8, D, dtype=F32),
            vm(N, D),
            vm(N, D),
            vm(N, D, dtype=F32),
            vm(2, N, H2W),
            pltpu.SemaphoreType.DMA((len(s.ag_chunks), 31)),
            pltpu.SemaphoreType.DMA((len(s.ag_chunks), 31)),
            pltpu.SemaphoreType.DMA((len(s.rs_chunks), 7)),
            pltpu.SemaphoreType.DMA((len(s.rs_chunks), 7)),
            pltpu.SemaphoreType.DMA((10,)),
            pltpu.SemaphoreType.DMA((10,)),
            pltpu.SemaphoreType.DMA((16,)),
            pltpu.SemaphoreType.DMA((2,)),
        ],
        compiler_params=pltpu.CompilerParams(
            collective_id=0, has_side_effects=True, vmem_limit_bytes=62 << 20
        ),
    )(
        tokens[0], cotangent[0], span_ids[0], gain_one[None], gain_two[None], b_out[None], b_down[None],
        b_up[None], *pieces,
    )
    out = list(out)
    if sub > 1:
        for i in range(2, 6):
            out[i] = lax.psum_scatter(
                out[i], "dp", scatter_dimension=out[i].ndim - 2, tiled=True, axis_index_groups=groups
            )
        out[6:] = lax.psum(tuple(out[6:]), "dp", axis_index_groups=groups)
    else:
        out = pl.pallas_call(
            functools.partial(deliver, len(results)),
            out_shape=results,
            in_specs=[any_space] * len(results),
            out_specs=[any_space] * len(results),
            scratch_shapes=[pltpu.VMEM(r.shape, r.dtype) for r in results]
            + [pltpu.SemaphoreType.DMA((len(results),))] * 2,
        )(*out)
    result, d_tokens, dq, do, du, dd, g1, g2, bo, bd, bu = out
    return (
        result[None],
        d_tokens[None],
        g1[0],
        jnp.transpose(dq, (1, 0, 2)),
        do.T,
        bo[0],
        g2[0],
        du,
        bu[0],
        dd.T,
        bd[0],
    )


def solution(mesh):
    in_specs = (
        P("dp", "tensor", None),
        P("dp", "tensor", None),
        P("dp", None, None),
        P(),
        P("dp", None, "tensor"),
        P("tensor", "dp"),
        P(),
        P(),
        P("dp", "tensor"),
        P("tensor"),
        P("tensor", "dp"),
        P(),
    )
    out_specs = (
        P("dp", "tensor", None),
        P("dp", "tensor", None),
        P(),
        P("dp", None, "tensor"),
        P("tensor", "dp"),
        P(),
        P(),
        P("dp", "tensor"),
        P(),
        P("tensor", "dp"),
        P(),
    )
    return jax.shard_map(shards, mesh=mesh, in_specs=in_specs, out_specs=out_specs, check_vma=False)
```

```python
import functools
import math

import jax
import jax.numpy as jnp
from jax import lax
from jax.experimental import pallas as pl
from jax.experimental.pallas import tpu as pltpu
from jax.sharding import PartitionSpec as P

HD = 64
BLK = 256
EPS = 1e-05
MASKED = -1e30
Z = 4
YX = 4
GROUPS = Z * YX
F32 = jnp.float32
BF = jnp.bfloat16
MESH = pl.DeviceIdType.MESH


def dot(a, b, ca, cb):
    return lax.dot_general(a, b, (((ca,), (cb,)), ((), ())), preferred_element_type=F32)


def nn(a, b):
    return dot(a, b, 1, 0)


def nt(a, b):
    return dot(a, b, 1, 1)


def tn(a, b):
    return dot(a, b, 0, 0)


def iota(shape, axis):
    return lax.broadcasted_iota(jnp.int32, shape, axis)


def unit_rows(values):
    centre = values - jnp.mean(values, axis=-1, keepdims=True)
    spread = jnp.mean(centre * centre, axis=-1, keepdims=True)
    inverse = lax.rsqrt(spread + EPS)
    return centre * inverse, inverse


def eight(values):
    return jnp.sum(values.reshape(values.shape[0] // 8, 8, values.shape[1]), axis=0)


class Sizes:
    pass


def kernel(s, *refs):
    (tok_in, cot_in, span, gain1, gain2, bout, bdown, bup_own, s_qkv, s_out, s_up, s_dn) = refs[:12]
    (res_out, dtok_out, g_qkv, g_out, g_up, g_dn, o_gain1, o_gain2, o_bout, o_bdown, o_bup) = refs[12:23]
    (W, G, R0, R1, R2, R3, H1, H1T, QKV, PT, O, MID, H2, H2T, COTT, HID, GI, GB, GBT,
     BUP, KSV, KSB, VSB, DSV, DSVR, SHARE, SPC, M8, BUACC, ACC, SM, SMR, tok, cot, RES, GO,
     ag_s, ag_r, rs_s, rs_r, sx_s, sx_r, lc, oc) = refs[23:]
    D, H2W, F2, NB = s.D, s.H2W, s.F2, s.NB
    QW = 3 * H2W
    FC, NFC = s.FC, F2 // s.FC
    C_OUT = QW

    def c_up(fc):
        return QW + H2W + 2 * FC * fc

    def c_dn(fc):
        return QW + H2W + 2 * FC * fc + FC

    d = lax.axis_index("dp")
    t = lax.axis_index("tensor")
    g = d // s.sub
    z = g // YX
    yx = g % YX
    rest = d % s.sub
    b2 = 2 - t
    b3 = 1 + t

    def at(zz, q):
        return ((zz * YX + q) * s.sub + rest, t)

    def flip(q, bit):
        y_bit, x_bit = q // 2, q % 2
        return jnp.where(bit == 2, (1 - y_bit) * 2 + x_bit, y_bit * 2 + 1 - x_bit)

    yx2 = flip(yx, b2)
    yx3 = flip(yx, b3)
    yx23 = 3 - yx
    pair = (d, 1 - t)
    peer2 = at(z, yx2)
    peer3 = at(z, yx3)
    zpeers = [at((z + k) % Z, yx) for k in range(1, Z)]

    barrier = pltpu.get_barrier_semaphore()
    for who in [pair, peer2, peer3] + zpeers:
        pl.semaphore_signal(barrier, inc=1, device_id=who, device_id_type=MESH)

    fetches = []

    def fetch(src, dst):
        cp = pltpu.make_async_copy(src, dst, lc.at[len(fetches)])
        cp.start()
        fetches.append(cp)

    own = W.at[t, z, yx]
    for j in range(3):
        for pr in range(2):
            fetch(s_qkv.at[j, :, pl.ds(128 * pr, 128)], own.at[:, pl.ds(384 * pr + 128 * j, 128)])
    fetch(s_out, own.at[:, pl.ds(C_OUT, H2W)])
    for fc in range(NFC):
        fetch(s_up.at[:, pl.ds(fc * FC, FC)], own.at[:, pl.ds(c_up(fc), FC)])
        fetch(s_dn.at[:, pl.ds(fc * FC, FC)], own.at[:, pl.ds(c_dn(fc), FC)])
    n_shards = len(fetches)
    fetch(tok_in, tok)
    fetch(cot_in, cot)
    BUP[t] = jnp.broadcast_to(bup_own[...], (8, F2))

    half_rows = iota((8, BLK), 0)
    for b in range(NB):
        line = span[pl.ds(t * NB + b, 1), :]
        belongs = jnp.logical_and(half_rows // NB == line, half_rows % NB == b)
        M8[:, b * BLK:(b + 1) * BLK] = belongs.astype(F32)
    SPC[...] = jnp.concatenate([span[...].astype(F32), jnp.zeros((120, BLK), F32)], axis=0).T
    zeros_in = (span[...] == 0).astype(F32)
    ones_in = (span[...] == 1).astype(F32)
    n_zero = jnp.sum(zeros_in, axis=1, keepdims=True)
    n_one = jnp.sum(ones_in, axis=1, keepdims=True)
    counts = jnp.concatenate(
        [n_zero[:NB], n_one[:NB], n_zero[NB:2 * NB], n_one[NB:2 * NB]], axis=0
    )
    log_counts = jnp.log(counts)
    own_counts = jnp.sum(M8[...], axis=1, keepdims=True)
    code = iota((16, 1), 0)
    block_of = (code // 8) * NB + code % NB

    for cp in fetches[:n_shards]:
        cp.wait()
    pl.semaphore_wait(barrier, 3 + Z - 1)

    def remote(src, dst, ss, rs, who):
        return pltpu.make_async_remote_copy(
            src_ref=src, dst_ref=dst, send_sem=ss, recv_sem=rs, device_id=who, device_id_type=MESH
        )

    chunks = s.ag_chunks
    group_of = {"o": yx, "2": yx2, "3": yx3, "23": yx23}
    kinds = ["z1", "z2", "z3"] + [a + str(k) for a in ("2s", "3s", "3t") for k in range(Z)]
    kinds += ["2g", "3g", "3h"] + ["p" + a for a in group_of]
    number = {kind: i for i, kind in enumerate(kinds)}

    def ag_copy(c, kind, got=False):
        lo, n = chunks[c]
        cols = pl.ds(lo, n)
        if kind[0] == "z":
            k = int(kind[1])
            window, who = W.at[t, (z + Z - k) % Z if got else z, yx, :, cols], zpeers[k - 1]
        elif kind[0] == "p":
            window, who = W.at[1 - t if got else t, :, group_of[kind[1:]], :, cols], pair
        else:
            there, here, who = {
                "2s": (yx2, yx, peer2), "3s": (yx3, yx, peer3), "3t": (yx23, yx2, peer3),
                "2g": (yx2, yx, peer2), "3g": (yx3, yx, peer3), "3h": (yx23, yx2, peer3),
            }[kind[:2]]
            group = there if got else here
            if len(kind) == 2:
                window = W.at[t, :, group, :, cols]
            else:
                window = W.at[t, (z + Z - int(kind[2])) % Z, group, :, cols]
        i = number[kind]
        return remote(window, window, ag_s.at[c, i], ag_r.at[c, i], who)

    def ag_done(place):
        for c in s.need[place]:
            for name in group_of:
                ag_copy(c, "p" + name, True).wait_recv()

    order = (1, 3, 2)
    after = (0, 1, 3, 2)

    def ag_events(fine):
        if not fine:
            return [
                ([], ["z1", "z3", "z2"]),
                (["z1", "z3", "z2"], ["2g", "3g", "po"]),
                (["2g"], ["3h", "p2"]),
                (["3g"], ["p3"]),
                (["3h"], ["p23"]),
            ]
        out = [([], ["z1", "z3", "z2", "2s0", "3s0"])]
        out += [([f"z{k}"], [f"2s{k}", f"3s{k}"] + (["po"] if k == 2 else [])) for k in order]
        out += [([f"2s{k}"], [f"3t{k}"] + (["p2"] if k == 2 else [])) for k in after]
        out += [([f"3s{k}" for k in after], ["p3"]), ([f"3t{k}" for k in after], ["p23"])]
        return out

    gathers = [ag_events(fine) for fine in s.ag_fine]

    def ag_event(c, step):
        arrived, starts = gathers[c][step]
        for kind in arrived:
            ag_copy(c, kind, True).wait_recv()
        for kind in starts:
            ag_copy(c, kind).start()

    def run(events):
        for kind, c, step in events:
            if kind == "a":
                ag_event(c, step)
            elif kind == "r":
                rs_steps[step](c)
            else:
                small_step(step)

    def in_slots(i, places):
        for when, events in enumerate(places):
            if events:
                @pl.when(i == when)
                def _():
                    run(events)

    def small_copy(i, src, dst, who):
        return remote(src, dst, sx_s.at[i], sx_r.at[i], who)

    def exchange(i, who):
        return small_copy(5 + i, SM.at[i], SMR.at[i], who)

    def small_step(i):
        whos = (pair, peer3, peer2)
        if i > 0:
            exchange(i - 1, whos[i - 1]).wait_recv()
            SM[i] = SM[i - 1] + SMR[i - 1]
        if i < 3:
            exchange(i, whos[i]).start()
        else:
            SMR[3 + z] = SM[3]
            for k in range(1, Z):
                small_copy(7 + k, SM.at[3], SMR.at[3 + z], zpeers[k - 1]).start()

    run(s.plan["first"])
    bup_copy = small_copy(0, BUP.at[t], BUP.at[t], pair)
    bup_copy.start()

    def wl(half, lo, n):
        return W[half, :, :, :, pl.ds(lo, n)].reshape(D, n)

    def rows_of(b, n=BLK):
        return pl.ds(pl.multiple_of(b * n, n), n)

    def loop(count, body, places=()):
        def step(i, _):
            body(i)
            in_slots(i, places)
            return 0

        lax.fori_loop(0, count, step, 0)


    for cp in fetches[n_shards:]:
        cp.wait()

    def norm_one(b, _):
        r = rows_of(b)
        unit, _inv = unit_rows(tok[r, :].astype(F32))
        low = (unit * gain1[...]).astype(BF)
        H1[r, :] = low
        H1T[:, r] = low.T
        COTT[:, r] = cot[r, :].T
        return 0

    lax.fori_loop(0, NB, norm_one, 0)

    BUACC[...] = jnp.zeros_like(BUACC)
    ACC[...] = jnp.zeros_like(ACC)
    DSV[...] = jnp.zeros_like(DSV)

    q_scale = jnp.where(iota((1, 384), 1) < 128, 1.0 / math.sqrt(HD), 1.0).astype(F32)
    member_low = jnp.concatenate([M8[...], M8[...]], axis=0).astype(BF)

    def ksv_copy(pr, got=False):
        window = KSV.at[pr, 1 - t if got else t]
        return small_copy(1 + pr, window, window, pair)

    def project(pr):
        lo = 384 * pr
        for half in range(2):
            QKV[half, :, lo:lo + 384] = (nn(H1[...], wl(half, lo, 384)) * q_scale).astype(BF)
        for half in range(2):
            sums = nn(member_low, QKV[half, :, lo + 128:lo + 384])[:8]
            KSV[pr, t, :, 256 * half:256 * half + 256] = (sums / own_counts).astype(BF).astype(F32)
        ksv_copy(pr).start()

    run(s.plan["second"])
    ag_done("second")
    project(0)
    run(s.plan["mid"])
    ag_done("mid")
    project(1)
    run(s.plan["third"])
    for pr in range(2):
        ksv_copy(pr, True).wait_recv()
        everything = KSV[pr].reshape(16, 512).astype(BF)
        for half in range(2):
            KSB[half, pr] = everything[:, 256 * half:256 * half + 128]
            VSB[half, pr] = everything[:, 256 * half + 128:256 * half + 256]

    even = iota((BLK, 128), 1) < HD

    def stacked(values):
        zero = jnp.zeros_like(values)
        return jnp.concatenate([jnp.where(even, values, zero), jnp.where(even, zero, values)], axis=0)

    def beside(values):
        return jnp.concatenate([values[:HD, :BLK], values[HD:, BLK:]], axis=0).astype(BF).T

    def part_of(half, pr, r, which):
        lo = 384 * pr + 128 * which
        return QKV[half, r, lo:lo + 128]

    def keys_of(half, pr, r):
        return jnp.concatenate([part_of(half, pr, r, 1), KSB[half, pr]], axis=0)

    def values_of(half, pr, r):
        return jnp.concatenate([part_of(half, pr, r, 2), VSB[half, pr]], axis=0)

    units = [(half, pr) for half in range(2) for pr in range(2)]

    def attend(b):
        r = rows_of(b)
        seen = block_of < t * NB + b
        scores = [nt(keys_of(half, pr, r), stacked(part_of(half, pr, r, 0))) for half, pr in units]
        probs = []
        for (half, pr), score in zip(units, scores):
            near = score[:BLK]
            far = jnp.where(seen, score[BLK:] + log_counts, MASKED)
            largest = jnp.maximum(jnp.max(near, axis=0, keepdims=True), jnp.max(far, axis=0, keepdims=True))
            near = jnp.exp(near - largest)
            far = jnp.exp(far - largest)
            inv = 1.0 / (jnp.sum(near, axis=0, keepdims=True) + jnp.sum(far, axis=0, keepdims=True))
            low = jnp.concatenate([(near * inv).astype(BF), (far * inv).astype(BF)], axis=0)
            PT[half, b, pr] = low
            probs.append(low)
        for (half, pr), low in zip(units, probs):
            O[half, r, 128 * pr:128 * pr + 128] = beside(tn(values_of(half, pr, r), low))

    loop(NB, attend, s.plan["attend"])

    run(s.plan["proj_wait"])
    ag_done("proj_wait")
    small_copy(0, BUP.at[1 - t], BUP.at[1 - t], pair).wait_recv()

    def out_proj(i):
        r = rows_of(i, s.big["proj"])
        branch = nt(O[0, r, :], wl(0, C_OUT, H2W)) + nt(O[1, r, :], wl(1, C_OUT, H2W))
        middle = tok[r, :].astype(F32) + (branch + bout[...])
        RES[r, :] = middle
        unit, _inv = unit_rows(middle)
        low = (unit * gain2[...]).astype(BF)
        H2[r, :] = low
        H2T[:, r] = low.T

    loop(s.rows // s.big["proj"], out_proj, s.plan["proj"])

    c0 = math.sqrt(2.0 / math.pi)
    c1 = c0 * 0.044715

    def feed(fc):
        cols = slice(fc * FC, (fc + 1) * FC)

        def one(i):
            r = rows_of(i, s.big["feed"])
            for half in range(2):
                x = nn(H2[r, :], wl(half, c_up(fc), FC)) + BUP[half, 0:1, cols]
                gh = nn(cot[r, :], wl(half, c_dn(fc), FC))
                sq = x * x
                th = jnp.tanh(x * (c0 + c1 * sq))
                up = 0.5 + 0.5 * th
                HID[half, r, cols] = (x * up).astype(BF)
                slope = up + (0.5 * x) * (1.0 - th * th) * (c0 + (3.0 * c1) * sq)
                gi = gh * slope
                GI[half, r, cols] = gi.astype(BF)
                BUACC[half, :, cols] += eight(gi)

        loop(s.rows // s.big["feed"], one, s.plan["feed" + str(fc)])

    def over_units(values, r, place):
        total = None
        for half in range(2):
            for fc in range(NFC):
                part = nt(values[half, r, fc * FC:(fc + 1) * FC], wl(half, place(fc), FC))
                total = part if total is None else total + part
        return total

    def feed_back(i):
        r = rows_of(i, s.big["feed_back"])
        g2 = over_units(GI, r, c_up)
        unit, inverse = unit_rows(RES[r, :])
        e = g2 * gain2[...]
        m1 = jnp.mean(e, axis=-1, keepdims=True)
        m2 = jnp.mean(e * unit, axis=-1, keepdims=True)
        grad_out = cot[r, :].astype(F32)
        mid = grad_out + inverse * (e - m1 - unit * m2)
        MID[r, :] = mid
        low = mid.astype(BF)
        GB[r, :] = low
        GBT[:, r] = low.T
        for half in range(2):
            GO[half, r, :] = nn(low, wl(half, C_OUT, H2W)).astype(BF)
        ACC[1] += eight(g2 * unit)
        ACC[2] += eight(mid)
        ACC[3] += eight(grad_out)

    def give(i):
        r = rows_of(i, s.big["give"])
        H1[r, :] = (RES[r, :] + (over_units(HID, r, c_dn) + bdown[...])).astype(BF)

    rchunks = s.rs_chunks

    def rs_copy(c, kind):
        lo, n = rchunks[c]
        cols = pl.ds(lo, n)
        if kind == 0:
            src, dst, who = G.at[1 - t, :, :, :, cols], R0.at[:, :, :, cols], pair
        elif kind == 1:
            src, dst, who = G.at[t, :, yx3, :, cols], R1.at[0, :, :, cols], peer3
        elif kind == 2:
            src, dst, who = G.at[t, :, yx23, :, cols], R1.at[1, :, :, cols], peer3
        elif kind == 3:
            src, dst, who = G.at[t, :, yx2, :, cols], R2.at[:, :, cols], peer2
        else:
            k = kind - 3
            src, dst, who = G.at[t, (z + k) % Z, yx, :, cols], R3.at[k - 1, :, cols], zpeers[k - 1]
        return remote(src, dst, rs_s.at[c, kind], rs_r.at[c, kind], who)

    def rs0(c):
        rs_copy(c, 0).start()

    def rs1(c):
        lo, n = rchunks[c]
        rs_copy(c, 0).wait_recv()
        cols = pl.ds(lo, n)

        def add(q):
            for zz in range(Z):
                G[t, zz, q, :, cols] = (
                    G[t, zz, q, :, cols].astype(F32) + R0[zz, q, :, cols].astype(F32)
                ).astype(BF)

        add(yx23)
        rs_copy(c, 2).start()
        add(yx3)
        rs_copy(c, 1).start()
        add(yx2)
        add(yx)

    def rs2(c):
        lo, n = rchunks[c]
        cols = pl.ds(lo, n)

        def add(q, j):
            for zz in range(Z):
                G[t, zz, q, :, cols] = (
                    G[t, zz, q, :, cols].astype(F32) + R1[j, zz, :, cols].astype(F32)
                ).astype(BF)

        rs_copy(c, 2).wait_recv()
        add(yx2, 1)
        rs_copy(c, 3).start()
        rs_copy(c, 1).wait_recv()
        add(yx, 0)

    def rs3(c):
        lo, n = rchunks[c]
        cols = pl.ds(lo, n)
        rs_copy(c, 3).wait_recv()
        for zz in range(Z):
            G[t, zz, yx, :, cols] = (
                G[t, zz, yx, :, cols].astype(F32) + R2[zz, :, cols].astype(F32)
            ).astype(BF)
        for kind in (4, 5, 6):
            rs_copy(c, kind).start()

    def rs4(c):
        lo, n = rchunks[c]
        cols = pl.ds(lo, n)
        total = G[t, z, yx, :, cols].astype(F32)
        for kind in (4, 5, 6):
            rs_copy(c, kind).wait_recv()
            total = total + R3[kind - 4, :, cols].astype(F32)
        total = total * s.factor
        if lo < QW:
            for piece in range(n // 128):
                pr, j = (lo // 128 + piece) // 3, (lo // 128 + piece) % 3
                g_qkv[j, :, 128 * pr:128 * pr + 128] = total[:, 128 * piece:128 * piece + 128]
        elif lo == C_OUT:
            g_out[...] = total
        else:
            for part in range(n // FC):
                place = (lo - QW - H2W) // FC + part
                dst = g_dn if place % 2 else g_up
                dst[:, (place // 2) * FC:(place // 2 + 1) * FC] = total[:, part * FC:(part + 1) * FC]

    rs_steps = (rs0, rs1, rs2, rs3, rs4)

    def weight_grad(lhs, rhs, lo, c_lo, n):
        for half in range(2):
            y = nn(lhs[...], rhs[half, :, lo:lo + n]).astype(BF)
            G[half, :, :, :, c_lo:c_lo + n] = y.reshape(Z, YX, D // GROUPS, n)

    for fc in range(NFC):
        run(s.plan["feed" + str(fc) + "_wait"])
        ag_done("feed" + str(fc) + "_wait")
        feed(fc)
        weight_grad(H2T, GI, fc * FC, c_up(fc), FC)
        run(s.plan["w" + str(2 * fc)])
        weight_grad(COTT, HID, fc * FC, c_dn(fc), FC)
        run(s.plan["w" + str(2 * fc + 1)])

    loop(s.rows // s.big["feed_back"], feed_back, s.plan["feed_back"])
    weight_grad(GBT, O, 0, C_OUT, H2W)
    run(s.plan["out"])

    GP = GI

    def attend_back(pr, i):
        places = [(b, half) for b in range(s.back) for half in range(2)]
        places = [(i * s.back + b, half) for b, half in places]
        grads = [stacked(GO[half, rows_of(b), 128 * pr:128 * pr + 128]) for b, half in places]
        dps = [nt(values_of(half, pr, rows_of(b)), up) for (b, half), up in zip(places, grads)]
        scores = []
        for (b, half), dp in zip(places, dps):
            p = PT[half, b, pr].astype(F32)
            corr = jnp.sum(p * dp, axis=0, keepdims=True)
            scores.append((p * (dp - corr)).astype(BF))
        lo = 384 * pr
        for (b, half), ds in zip(places, scores):
            r = rows_of(b)
            dk = nn(ds, stacked(part_of(half, pr, r, 0)))
            GP[half, r, lo + 128:lo + 256] = dk[:BLK].astype(BF)
            DSV[pr, :, :, 256 * half:256 * half + 128] += dk[BLK:].reshape(2, 8, 128)
        for (b, half), ds in zip(places, scores):
            r = rows_of(b)
            GP[half, r, lo:lo + 128] = beside(tn(keys_of(half, pr, r), ds) * (1.0 / math.sqrt(HD)))
        for (b, half), up in zip(places, grads):
            dv = nn(PT[half, b, pr], up)
            GP[half, rows_of(b), lo + 256:lo + 384] = dv[:BLK].astype(BF)
            DSV[pr, :, :, 256 * half + 128:256 * half + 256] += dv[BLK:].reshape(2, 8, 128)

    span_lane = iota((BLK, 128), 1)

    def dsv_copy(pr):
        return small_copy(3 + pr, DSV.at[pr, 1 - t], DSVR.at[pr], pair)

    def shared(pr):
        dsv_copy(pr).wait_recv()
        SHARE[pr] = (DSV[pr, t] + DSVR[pr]) / own_counts
        lo = 384 * pr

        def spread(b):
            r = rows_of(b)
            column = jnp.sum(jnp.where(span_lane == t * NB + b, SPC[...], 0.0), axis=1, keepdims=True)
            first = column == 0.0
            for half in range(2):
                lanes = slice(256 * half, 256 * half + 256)
                add = jnp.where(first, SHARE[pr, pl.ds(b, 1), lanes], SHARE[pr, pl.ds(NB + b, 1), lanes])
                GP[half, r, lo + 128:lo + 384] = (GP[half, r, lo + 128:lo + 384].astype(F32) + add).astype(BF)

        loop(NB, spread)

    loop(NB // s.back, functools.partial(attend_back, 0), s.plan["back0"])
    dsv_copy(0).start()
    run(s.plan["share0"])
    shared(0)
    weight_grad(H1T, GP, 0, 0, 384)
    run(s.plan["q0"])
    loop(NB // s.back, functools.partial(attend_back, 1), s.plan["back1"])
    dsv_copy(1).start()
    weight_grad(H1T, GP, 384, 384, 128)
    run(s.plan["share1"])
    shared(1)
    weight_grad(H1T, GP, 512, 512, 256)
    run(s.plan["q1"])

    def last(i):
        r = rows_of(i, s.big["last"])
        grad = nt(GP[0, r, 0:QW], wl(0, 0, QW)) + nt(GP[1, r, 0:QW], wl(1, 0, QW))
        unit, inverse = unit_rows(tok[r, :].astype(F32))
        e = grad * gain1[...]
        m1 = jnp.mean(e, axis=-1, keepdims=True)
        m2 = jnp.mean(e * unit, axis=-1, keepdims=True)
        H2[r, :] = (MID[r, :] + inverse * (e - m1 - unit * m2)).astype(BF)
        ACC[0] += eight(grad * unit)

    loop(s.rows // s.big["last"], last, s.plan["last"])
    out_copies = [pltpu.make_async_copy(H2, dtok_out, oc.at[0]), pltpu.make_async_copy(H1, res_out, oc.at[1])]
    out_copies[0].start()

    folded = [jnp.sum(ACC[j], axis=0, keepdims=True) for j in range(4)]
    for half in range(2):
        line = jnp.sum(BUACC[half], axis=0, keepdims=True)
        folded += [line[:, j * D:(j + 1) * D] for j in range(F2 // D)]
    SM[0] = jnp.concatenate(folded, axis=0)

    run(s.plan["small"])
    loop(s.rows // s.big["give"], give, s.plan["give"])
    out_copies[1].start()
    run(s.plan["end"])
    for k in range(1, Z):
        small_copy(7 + k, SM.at[3], SMR.at[3 + (z + Z - k) % Z], zpeers[k - 1]).wait_recv()
    summed = (SMR[3] + SMR[4] + SMR[5] + SMR[6]) * s.factor
    o_gain1[...] = summed[0:1]
    o_gain2[...] = summed[1:2]
    o_bout[...] = summed[2:3]
    o_bdown[...] = summed[3:4]
    for j in range(2 * F2 // D):
        o_bup[:, j * D:(j + 1) * D] = summed[4 + j:5 + j]


    for cp in out_copies:
        cp.wait()
    for c in range(len(chunks)):
        for _arrived, starts in gathers[c]:
            for kind in starts:
                ag_copy(c, kind).wait_send()
    for c in range(len(rchunks)):
        for kind in range(7):
            rs_copy(c, kind).wait_send()
    bup_copy.wait_send()
    for pr in range(2):
        ksv_copy(pr).wait_send()
        dsv_copy(pr).wait_send()
    for i, who in enumerate((pair, peer3, peer2)):
        exchange(i, who).wait_send()
    for k in range(1, Z):
        small_copy(7 + k, SM.at[3], SMR.at[3 + z], zpeers[k - 1]).wait_send()


def deliver(n, *refs):
    ins, outs, held, (got, sent) = refs[:n], refs[n:2 * n], refs[2 * n:3 * n], refs[3 * n:]
    firsts = [pltpu.make_async_copy(ins[i], held[i], got.at[i]) for i in range(n)]
    seconds = [pltpu.make_async_copy(held[i], outs[i], sent.at[i]) for i in range(n)]
    for cp in firsts:
        cp.start()
    for first, second in zip(firsts, seconds):
        first.wait()
        second.start()
    for cp in seconds:
        cp.wait()


def shards(
    tokens, cotangent, span_ids, gain_one, w_qkv, w_out, b_out, gain_two, w_up, b_up, w_down, b_down
):
    s = Sizes()
    dp = lax.axis_size("dp")
    s.sub = dp // GROUPS
    s.D = tokens.shape[2]
    s.rows = tokens.shape[1]
    s.NB = s.rows // BLK
    s.H2W = w_qkv.shape[2]
    s.F2 = w_up.shape[1]
    s.factor = 1.0 / math.sqrt(dp * lax.axis_size("tensor") * s.rows)
    sub, D, H2W, F2, N, NB = s.sub, s.D, s.H2W, s.F2, s.rows, s.NB
    QW = 3 * H2W
    width = QW + H2W + 2 * F2
    s.FC = 512
    s.FC = 512
    s.big = {'proj': 512, 'feed': 512, 'feed_back': 512, 'last': 512, 'give': 512}
    s.back = 2
    s.ag_chunks = [(0, 384), (384, 384), (768, 1280), (2048, 1024)]
    s.ag_fine = (1, 1, 1, 1)
    s.need = {'second': (0,), 'mid': (1,), 'proj_wait': (2,), 'feed0_wait': (), 'feed1_wait': (3,)}
    s.rs_chunks = [(1024, 512), (1536, 512), (2048, 512), (2560, 512), (768, 256), (0, 384), (384, 128), (512, 256)]
    s.plan = {
        "first": (('a', 0, 0), ('a', 1, 0), ('a', 2, 0), ),
        "second": (('a', 0, 4), ('a', 1, 4), ('a', 0, 1), ('a', 0, 2), ('a', 2, 4), ('a', 0, 3), ('a', 1, 1), ('a', 1, 2), ('a', 0, 5), ('a', 0, 6), ('a', 1, 3), ('a', 0, 7), ('a', 3, 0), ('a', 0, 8), ('a', 2, 1), ('a', 1, 5), ('a', 1, 6), ('a', 1, 7), ('a', 2, 2), ('a', 1, 8), ('a', 0, 9), ('a', 3, 4), ),
        "mid": (('a', 2, 5), ('a', 2, 3), ('a', 1, 9), ('a', 3, 1), ('a', 2, 6), ('a', 3, 2), ),
        "third": (),
        "proj_wait": (('a', 2, 9), ('a', 3, 7), ('a', 3, 8), ),
        "feed0_wait": (),
        "feed1_wait": (),
        "w0": (('r', 0, 0), ),
        "w1": (('r', 1, 0), ),
        "w2": (('r', 2, 0), ),
        "w3": (('r', 3, 0), ),
        "out": (('r', 4, 0), ),
        "share0": (),
        "q0": (('r', 5, 0), ),
        "share1": (('r', 6, 0), ),
        "q1": (('r', 7, 0), ('r', 2, 3), ),
        "small": (('s', 0, 0), ),
        "end": (('r', 7, 2), ('r', 2, 4), ('r', 5, 3), ('s', 0, 2), ('r', 6, 3), ('r', 3, 4), ('r', 7, 3), ('s', 0, 3), ('r', 4, 4), ('r', 5, 4), ('r', 6, 4), ('r', 7, 4), ),
        "attend": (
            (('a', 2, 7), ('a', 3, 3), ),
            (('a', 2, 8), ('a', 3, 5), ),
            (),
            (('a', 3, 6), ),
        ),
        "proj": (
            (),
            (),
        ),
        "feed0": (
            (('a', 3, 9), ),
            (),
        ),
        "feed1": (
            (('r', 0, 1), ),
            (('r', 1, 1), ),
        ),
        "feed_back": (
            (('r', 0, 2), ('r', 2, 1), ),
            (('r', 3, 1), ('r', 1, 2), ),
        ),
        "back0": (
            (('r', 0, 3), ),
            (('r', 4, 1), ('r', 2, 2), ),
        ),
        "back1": (
            (('r', 3, 2), ),
            (('r', 1, 3), ('r', 5, 1), ('r', 0, 4), ('r', 4, 2), ),
        ),
        "last": (
            (('r', 6, 1), ('r', 3, 3), ),
            (('r', 7, 1), ('r', 5, 2), ),
        ),
        "give": (
            (('r', 4, 3), ),
            (('r', 1, 4), ('s', 0, 1), ('r', 6, 2), ),
        ),
    }
    groups = [[a * sub + b for b in range(sub)] for a in range(dp // sub)]
    pieces = [jnp.transpose(w_qkv, (1, 0, 2)), w_out.T, w_up, w_down.T]
    if sub > 1:
        pieces = [
            lax.all_gather(piece, "dp", axis=piece.ndim - 2, tiled=True, axis_index_groups=groups)
            for piece in pieces
        ]
    R = D // GROUPS

    def vm(*shape, dtype=BF):
        return pltpu.VMEM(shape, dtype)

    any_space = pl.BlockSpec(memory_space=pl.ANY)
    in_vmem = pl.BlockSpec(memory_space=pltpu.VMEM)
    results = (
        jax.ShapeDtypeStruct((N, D), BF),
        jax.ShapeDtypeStruct((N, D), BF),
        jax.ShapeDtypeStruct((3, R, H2W), F32),
        jax.ShapeDtypeStruct((R, H2W), F32),
        jax.ShapeDtypeStruct((R, F2), F32),
        jax.ShapeDtypeStruct((R, F2), F32),
        jax.ShapeDtypeStruct((1, D), F32),
        jax.ShapeDtypeStruct((1, D), F32),
        jax.ShapeDtypeStruct((1, D), F32),
        jax.ShapeDtypeStruct((1, D), F32),
        jax.ShapeDtypeStruct((1, 2 * F2), F32),
    )
    out = pl.pallas_call(
        functools.partial(kernel, s),
        out_shape=results,
        in_specs=[any_space] * 2 + [in_vmem] * 6 + [any_space] * 4,
        out_specs=[any_space] * 2 + [in_vmem] * 9,
        scratch_shapes=[
            vm(2, Z, YX, R, width),
            vm(2, Z, YX, R, width),
            vm(Z, YX, R, width),
            vm(2, Z, R, width),
            vm(Z, R, width),
            vm(Z - 1, R, width),
            vm(N, D),
            vm(D, N),
            vm(2, N, QW),
            vm(2, NB, 2, BLK + 16, 2 * BLK),
            vm(2, N, H2W),
            vm(N, D, dtype=F32),
            vm(N, D),
            vm(D, N),
            vm(D, N),
            vm(2, N, F2),
            vm(2, N, F2),
            vm(N, D),
            vm(D, N),
            vm(2, 8, F2, dtype=F32),
            vm(2, 2, 8, 512, dtype=F32),
            vm(2, 2, 16, 128),
            vm(2, 2, 16, 128),
            vm(2, 2, 8, 512, dtype=F32),
            vm(2, 8, 512, dtype=F32),
            vm(2, 8, 512, dtype=F32),
            vm(BLK, 128, dtype=F32),
            vm(8, N, dtype=F32),
            vm(2, 8, F2, dtype=F32),
            vm(4, 8, D, dtype=F32),
            vm(4, 8, D, dtype=F32),
            vm(7, 8, D, dtype=F32),
            vm(N, D),
            vm(N, D),
            vm(N, D, dtype=F32),
            vm(2, N, H2W),
            pltpu.SemaphoreType.DMA((len(s.ag_chunks), 22)),
            pltpu.SemaphoreType.DMA((len(s.ag_chunks), 22)),
            pltpu.SemaphoreType.DMA((len(s.rs_chunks), 7)),
            pltpu.SemaphoreType.DMA((len(s.rs_chunks), 7)),
            pltpu.SemaphoreType.DMA((11,)),
            pltpu.SemaphoreType.DMA((11,)),
            pltpu.SemaphoreType.DMA((16,)),
            pltpu.SemaphoreType.DMA((2,)),
        ],
        compiler_params=pltpu.CompilerParams(
            collective_id=0, has_side_effects=True, vmem_limit_bytes=62 << 20
        ),
    )(
        tokens[0], cotangent[0], span_ids[0], gain_one[None], gain_two[None], b_out[None], b_down[None],
        b_up[None], *pieces,
    )
    out = list(out)
    if sub > 1:
        for i in range(2, 6):
            out[i] = lax.psum_scatter(
                out[i], "dp", scatter_dimension=out[i].ndim - 2, tiled=True, axis_index_groups=groups
            )
        out[6:] = lax.psum(tuple(out[6:]), "dp", axis_index_groups=groups)
    else:
        out = pl.pallas_call(
            functools.partial(deliver, len(results)),
            out_shape=results,
            in_specs=[any_space] * len(results),
            out_specs=[any_space] * len(results),
            scratch_shapes=[pltpu.VMEM(r.shape, r.dtype) for r in results]
            + [pltpu.SemaphoreType.DMA((len(results),))] * 2,
        )(*out)
    result, d_tokens, dq, do, du, dd, g1, g2, bo, bd, bu = out
    return (
        result[None],
        d_tokens[None],
        g1[0],
        jnp.transpose(dq, (1, 0, 2)),
        do.T,
        bo[0],
        g2[0],
        du,
        bu[0],
        dd.T,
        bd[0],
    )


def solution(mesh):
    in_specs = (
        P("dp", "tensor", None),
        P("dp", "tensor", None),
        P("dp", None, None),
        P(),
        P("dp", None, "tensor"),
        P("tensor", "dp"),
        P(),
        P(),
        P("dp", "tensor"),
        P("tensor"),
        P("tensor", "dp"),
        P(),
    )
    out_specs = (
        P("dp", "tensor", None),
        P("dp", "tensor", None),
        P(),
        P("dp", None, "tensor"),
        P("tensor", "dp"),
        P(),
        P(),
        P("dp", "tensor"),
        P(),
        P("tensor", "dp"),
        P(),
    )
    return jax.shard_map(shards, mesh=mesh, in_specs=in_specs, out_specs=out_specs, check_vma=False)
```

```python
import functools
import math

import jax
import jax.numpy as jnp
from jax import lax
from jax.experimental import pallas as pl
from jax.experimental.pallas import tpu as pltpu
from jax.sharding import PartitionSpec as P

HD = 64
BLK = 256
EPS = 1e-05
MASKED = -1e30
Z = 4
YX = 4
GROUPS = Z * YX
F32 = jnp.float32
BF = jnp.bfloat16
MESH = pl.DeviceIdType.MESH


def dot(a, b, ca, cb):
    return lax.dot_general(a, b, (((ca,), (cb,)), ((), ())), preferred_element_type=F32)


def nn(a, b):
    return dot(a, b, 1, 0)


def nt(a, b):
    return dot(a, b, 1, 1)


def tn(a, b):
    return dot(a, b, 0, 0)


def iota(shape, axis):
    return lax.broadcasted_iota(jnp.int32, shape, axis)


def unit_rows(values):
    centre = values - jnp.mean(values, axis=-1, keepdims=True)
    spread = jnp.mean(centre * centre, axis=-1, keepdims=True)
    inverse = lax.rsqrt(spread + EPS)
    return centre * inverse, inverse


def eight(values):
    return jnp.sum(values.reshape(values.shape[0] // 8, 8, values.shape[1]), axis=0)


class Sizes:
    pass


def kernel(s, *refs):
    (tok_in, cot_in, span_in, gain1_in, gain2_in, bout_in, bdown_in, bup_in, s_qkv, s_out, s_up, s_dn) = refs[:12]
    (res_out, dtok_out, g_qkv, g_out, g_up, g_dn, o_gain1, o_gain2, o_bout, o_bdown, o_bup) = refs[12:23]
    (W, G, R0, R1, R2, R3, H1, H1T, QKV, PT, O, MID, H2, H2T, COTT, HID, GI, GB, GBT,
     BUP, KSV, KSB, VSB, DSV, DSVR, SHARE, GAINS, SPC, M8, BUACC, ACC, SM, SMR, tok, cot, RES, GO,
     span, gain1, gain2, bout, bdown, bup_own,
     ag_s, ag_r, rs_s, rs_r, sx_s, sx_r, lc, oc) = refs[23:]
    D, H2W, F2, NB = s.D, s.H2W, s.F2, s.NB
    QW = 3 * H2W
    FC, NFC = s.FC, F2 // s.FC
    C_OUT = QW

    def c_up(fc):
        return QW + H2W + 2 * FC * fc

    def c_dn(fc):
        return QW + H2W + 2 * FC * fc + FC

    d = lax.axis_index("dp")
    t = lax.axis_index("tensor")
    g = d // s.sub
    z = g // YX
    yx = g % YX
    rest = d % s.sub
    b2 = 2 - t
    b3 = 1 + t

    def at(zz, q):
        return ((zz * YX + q) * s.sub + rest, t)

    def flip(q, bit):
        y_bit, x_bit = q // 2, q % 2
        return jnp.where(bit == 2, (1 - y_bit) * 2 + x_bit, y_bit * 2 + 1 - x_bit)

    yx2 = flip(yx, b2)
    yx3 = flip(yx, b3)
    yx23 = 3 - yx
    pair = (d, 1 - t)
    peer2 = at(z, yx2)
    peer3 = at(z, yx3)
    zpeers = [at((z + k) % Z, yx) for k in range(1, Z)]

    barrier = pltpu.get_barrier_semaphore()
    for who in [pair, peer2, peer3] + zpeers:
        pl.semaphore_signal(barrier, inc=1, device_id=who, device_id_type=MESH)

    fetches = []

    def fetch(src, dst):
        cp = pltpu.make_async_copy(src, dst, lc.at[len(fetches)])
        cp.start()
        fetches.append(cp)

    fetch(span_in, span)
    fetch(bup_in, bup_own)
    own = W.at[t, z, yx]
    for j in range(3):
        for pr in range(2):
            fetch(s_qkv.at[j, :, pl.ds(128 * pr, 128)], own.at[:, pl.ds(384 * pr + 128 * j, 128)])
    fetch(s_out, own.at[:, pl.ds(C_OUT, H2W)])
    for fc in range(NFC):
        fetch(s_up.at[:, pl.ds(fc * FC, FC)], own.at[:, pl.ds(c_up(fc), FC)])
        fetch(s_dn.at[:, pl.ds(fc * FC, FC)], own.at[:, pl.ds(c_dn(fc), FC)])
    n_shards = len(fetches)
    for src, dst in ((gain1_in, gain1), (gain2_in, gain2), (bout_in, bout), (bdown_in, bdown)):
        fetch(src, dst)
    fetch(tok_in, tok)
    fetch(cot_in, cot)
    for cp in fetches[:2]:
        cp.wait()
    BUP[t] = jnp.broadcast_to(bup_own[...], (8, F2))

    half_rows = iota((8, BLK), 0)
    for b in range(NB):
        line = span[pl.ds(t * NB + b, 1), :]
        belongs = jnp.logical_and(half_rows // NB == line, half_rows % NB == b)
        M8[:, b * BLK:(b + 1) * BLK] = belongs.astype(F32)
    SPC[...] = jnp.concatenate([span[...].astype(F32), jnp.zeros((120, BLK), F32)], axis=0).T
    zeros_in = (span[...] == 0).astype(F32)
    ones_in = (span[...] == 1).astype(F32)
    n_zero = jnp.sum(zeros_in, axis=1, keepdims=True)
    n_one = jnp.sum(ones_in, axis=1, keepdims=True)
    counts = jnp.concatenate(
        [n_zero[:NB], n_one[:NB], n_zero[NB:2 * NB], n_one[NB:2 * NB]], axis=0
    )
    log_counts = jnp.log(counts)
    own_counts = jnp.sum(M8[...], axis=1, keepdims=True)
    code = iota((16, 1), 0)
    block_of = (code // 8) * NB + code % NB

    for cp in fetches[2:n_shards]:
        cp.wait()
    pl.semaphore_wait(barrier, 3 + Z - 1)

    def remote(src, dst, ss, rs, who):
        return pltpu.make_async_remote_copy(
            src_ref=src, dst_ref=dst, send_sem=ss, recv_sem=rs, device_id=who, device_id_type=MESH
        )

    chunks = s.ag_chunks
    group_of = {"o": yx, "2": yx2, "3": yx3, "23": yx23}
    kinds = ["z1", "z2", "z3"] + [a + str(k) for a in ("2s", "3s", "3t") for k in range(Z)]
    kinds += ["2g", "3g", "3h"] + ["p" + a for a in group_of]
    number = {kind: i for i, kind in enumerate(kinds)}

    def ag_copy(c, kind, got=False):
        lo, n = chunks[c]
        cols = pl.ds(lo, n)
        if kind[0] == "z":
            k = int(kind[1])
            window, who = W.at[t, (z + Z - k) % Z if got else z, yx, :, cols], zpeers[k - 1]
        elif kind[0] == "p":
            window, who = W.at[1 - t if got else t, :, group_of[kind[1:]], :, cols], pair
        else:
            there, here, who = {
                "2s": (yx2, yx, peer2), "3s": (yx3, yx, peer3), "3t": (yx23, yx2, peer3),
                "2g": (yx2, yx, peer2), "3g": (yx3, yx, peer3), "3h": (yx23, yx2, peer3),
            }[kind[:2]]
            group = there if got else here
            if len(kind) == 2:
                window = W.at[t, :, group, :, cols]
            else:
                window = W.at[t, (z + Z - int(kind[2])) % Z, group, :, cols]
        i = number[kind]
        return remote(window, window, ag_s.at[c, i], ag_r.at[c, i], who)

    def ag_done(place):
        for c in s.need[place]:
            for name in group_of:
                ag_copy(c, "p" + name, True).wait_recv()

    order = (1, 3, 2)
    after = (0, 1, 3, 2)

    def ag_events(fine):
        if not fine:
            return [
                ([], ["z1", "z3", "z2"]),
                (["z1", "z3", "z2"], ["2g", "3g", "po"]),
                (["2g"], ["3h", "p2"]),
                (["3g"], ["p3"]),
                (["3h"], ["p23"]),
            ]
        out = [([], ["z1", "z3", "z2", "2s0", "3s0"])]
        out += [([f"z{k}"], [f"2s{k}", f"3s{k}"] + (["po"] if k == 2 else [])) for k in order]
        out += [([f"2s{k}"], [f"3t{k}"] + (["p2"] if k == 2 else [])) for k in after]
        out += [([f"3s{k}" for k in after], ["p3"]), ([f"3t{k}" for k in after], ["p23"])]
        return out

    gathers = [ag_events(fine) for fine in s.ag_fine]

    def ag_event(c, step):
        arrived, starts = gathers[c][step]
        for kind in arrived:
            ag_copy(c, kind, True).wait_recv()
        for kind in starts:
            ag_copy(c, kind).start()

    def run(events):
        for kind, c, step in events:
            if kind == "a":
                ag_event(c, step)
            elif kind == "r":
                rs_steps[step](c)
            else:
                small_step(step)

    def in_slots(i, places):
        for when, events in enumerate(places):
            if events:
                @pl.when(i == when)
                def _():
                    run(events)

    def small_copy(i, src, dst, who):
        return remote(src, dst, sx_s.at[i], sx_r.at[i], who)

    def exchange(i, who):
        return small_copy(5 + i, SM.at[i], SMR.at[i], who)

    def small_step(i):
        whos = (pair, peer3, peer2)
        if i > 0:
            exchange(i - 1, whos[i - 1]).wait_recv()
            SM[i] = SM[i - 1] + SMR[i - 1]
        if i < 3:
            exchange(i, whos[i]).start()
        else:
            SMR[3 + z] = SM[3]
            for k in range(1, Z):
                small_copy(7 + k, SM.at[3], SMR.at[3 + z], zpeers[k - 1]).start()

    run(s.plan["first"])
    bup_copy = small_copy(0, BUP.at[t], BUP.at[t], pair)
    bup_copy.start()

    def wl(half, lo, n):
        return W[half, :, :, :, pl.ds(lo, n)].reshape(D, n)

    def rows_of(b, n=BLK):
        return pl.ds(pl.multiple_of(b * n, n), n)

    def loop(count, body, places=()):
        def step(i, _):
            body(i)
            in_slots(i, places)
            return 0

        lax.fori_loop(0, count, step, 0)


    for cp in fetches[n_shards:]:
        cp.wait()

    def norm_one(b, _):
        r = rows_of(b)
        unit, _inv = unit_rows(tok[r, :].astype(F32))
        low = (unit * gain1[...]).astype(BF)
        H1[r, :] = low
        H1T[:, r] = low.T
        COTT[:, r] = cot[r, :].T
        return 0

    lax.fori_loop(0, NB, norm_one, 0)

    BUACC[...] = jnp.zeros_like(BUACC)
    ACC[...] = jnp.zeros_like(ACC)
    GAINS[...] = jnp.zeros_like(GAINS)
    DSV[...] = jnp.zeros_like(DSV)

    q_scale = jnp.where(iota((1, 384), 1) < 128, 1.0 / math.sqrt(HD), 1.0).astype(F32)
    member_low = jnp.concatenate([M8[...], M8[...]], axis=0).astype(BF)

    def ksv_copy(pr, got=False):
        window = KSV.at[pr, 1 - t if got else t]
        return small_copy(1 + pr, window, window, pair)

    def project(pr):
        lo = 384 * pr
        for half in range(2):
            QKV[half, :, lo:lo + 384] = (nn(H1[...], wl(half, lo, 384)) * q_scale).astype(BF)
        for half in range(2):
            sums = nn(member_low, QKV[half, :, lo + 128:lo + 384])[:8]
            KSV[pr, t, :, 256 * half:256 * half + 256] = (sums / own_counts).astype(BF).astype(F32)
        ksv_copy(pr).start()

    run(s.plan["second"])
    ag_done("second")
    project(0)
    run(s.plan["mid"])
    ag_done("mid")
    project(1)
    run(s.plan["third"])
    for pr in range(2):
        ksv_copy(pr, True).wait_recv()
        everything = KSV[pr].reshape(16, 512).astype(BF)
        for half in range(2):
            KSB[half, pr] = everything[:, 256 * half:256 * half + 128]
            VSB[half, pr] = everything[:, 256 * half + 128:256 * half + 256]

    even = iota((BLK, 128), 1) < HD

    def stacked(values):
        zero = jnp.zeros_like(values)
        return jnp.concatenate([jnp.where(even, values, zero), jnp.where(even, zero, values)], axis=0)

    def beside(values):
        return jnp.concatenate([values[:HD, :BLK], values[HD:, BLK:]], axis=0).astype(BF).T

    def part_of(half, pr, r, which):
        lo = 384 * pr + 128 * which
        return QKV[half, r, lo:lo + 128]

    def keys_of(half, pr, r):
        return jnp.concatenate([part_of(half, pr, r, 1), KSB[half, pr]], axis=0)

    def values_of(half, pr, r):
        return jnp.concatenate([part_of(half, pr, r, 2), VSB[half, pr]], axis=0)

    units = [(half, pr) for half in range(2) for pr in range(2)]

    def attend(b):
        r = rows_of(b)
        seen = block_of < t * NB + b
        scores = [nt(keys_of(half, pr, r), stacked(part_of(half, pr, r, 0))) for half, pr in units]
        probs = []
        for (half, pr), score in zip(units, scores):
            near = score[:BLK]
            far = jnp.where(seen, score[BLK:] + log_counts, MASKED)
            largest = jnp.maximum(jnp.max(near, axis=0, keepdims=True), jnp.max(far, axis=0, keepdims=True))
            near = jnp.exp(near - largest)
            far = jnp.exp(far - largest)
            inv = 1.0 / (jnp.sum(near, axis=0, keepdims=True) + jnp.sum(far, axis=0, keepdims=True))
            low = jnp.concatenate([(near * inv).astype(BF), (far * inv).astype(BF)], axis=0)
            PT[half, b, pr] = low
            probs.append(low)
        for (half, pr), low in zip(units, probs):
            O[half, r, 128 * pr:128 * pr + 128] = beside(tn(values_of(half, pr, r), low))

    loop(NB, attend, s.plan["attend"])

    run(s.plan["proj_wait"])
    ag_done("proj_wait")
    small_copy(0, BUP.at[1 - t], BUP.at[1 - t], pair).wait_recv()

    def out_proj(i):
        r = rows_of(i, s.big["proj"])
        branch = nt(O[0, r, :], wl(0, C_OUT, H2W)) + nt(O[1, r, :], wl(1, C_OUT, H2W))
        middle = tok[r, :].astype(F32) + (branch + bout[...])
        RES[r, :] = middle
        unit, _inv = unit_rows(middle)
        low = (unit * gain2[...]).astype(BF)
        H2[r, :] = low
        H2T[:, r] = low.T

    loop(s.rows // s.big["proj"], out_proj, s.plan["proj"])

    c0 = math.sqrt(2.0 / math.pi)
    c1 = c0 * 0.044715

    def feed(fc):
        cols = slice(fc * FC, (fc + 1) * FC)

        def one(i):
            r = rows_of(i, s.big["feed"])
            for half in range(2):
                x = nn(H2[r, :], wl(half, c_up(fc), FC)) + BUP[half, 0:1, cols]
                gh = nn(cot[r, :], wl(half, c_dn(fc), FC))
                sq = x * x
                th = jnp.tanh(x * (c0 + c1 * sq))
                up = 0.5 + 0.5 * th
                HID[half, r, cols] = (x * up).astype(BF)
                slope = up + (0.5 * x) * (1.0 - th * th) * (c0 + (3.0 * c1) * sq)
                gi = gh * slope
                GI[half, r, cols] = gi.astype(BF)
                BUACC[half, :, cols] += eight(gi)

        loop(s.rows // s.big["feed"], one, s.plan["feed" + str(fc)])

    def over_units(values, r, place):
        total = None
        for half in range(2):
            for fc in range(NFC):
                part = nt(values[half, r, fc * FC:(fc + 1) * FC], wl(half, place(fc), FC))
                total = part if total is None else total + part
        return total

    def feed_back(i):
        r = rows_of(i, s.big["feed_back"])
        g2 = over_units(GI, r, c_up)
        unit, inverse = unit_rows(RES[r, :])
        e = g2 * gain2[...]
        m1 = jnp.mean(e, axis=-1, keepdims=True)
        m2 = jnp.mean(e * unit, axis=-1, keepdims=True)
        grad_out = cot[r, :].astype(F32)
        mid = grad_out + inverse * (e - m1 - unit * m2)
        MID[r, :] = mid
        low = mid.astype(BF)
        GB[r, :] = low
        GBT[:, r] = low.T
        for half in range(2):
            GO[half, r, :] = nn(low, wl(half, C_OUT, H2W)).astype(BF)
        ACC[1] += eight(g2 * unit)
        ACC[2] += eight(mid)
        ACC[3] += eight(grad_out)

    def give(i):
        r = rows_of(i, s.big["give"])
        H1[r, :] = (RES[r, :] + (over_units(HID, r, c_dn) + bdown[...])).astype(BF)

    rchunks = s.rs_chunks

    def rs_copy(c, kind):
        lo, n = rchunks[c]
        cols = pl.ds(lo, n)
        if kind == 0:
            src, dst, who = G.at[1 - t, :, :, :, cols], R0.at[:, :, :, cols], pair
        elif kind == 1:
            src, dst, who = G.at[t, :, yx3, :, cols], R1.at[0, :, :, cols], peer3
        elif kind == 2:
            src, dst, who = G.at[t, :, yx23, :, cols], R1.at[1, :, :, cols], peer3
        elif kind == 3:
            src, dst, who = G.at[t, :, yx2, :, cols], R2.at[:, :, cols], peer2
        else:
            k = kind - 3
            src, dst, who = G.at[t, (z + k) % Z, yx, :, cols], R3.at[k - 1, :, cols], zpeers[k - 1]
        return remote(src, dst, rs_s.at[c, kind], rs_r.at[c, kind], who)

    def rs0(c):
        rs_copy(c, 0).start()

    def rs1(c):
        lo, n = rchunks[c]
        rs_copy(c, 0).wait_recv()
        cols = pl.ds(lo, n)

        def add(q):
            for zz in range(Z):
                G[t, zz, q, :, cols] = (
                    G[t, zz, q, :, cols].astype(F32) + R0[zz, q, :, cols].astype(F32)
                ).astype(BF)

        add(yx23)
        rs_copy(c, 2).start()
        add(yx3)
        rs_copy(c, 1).start()
        add(yx2)
        add(yx)

    def rs2(c):
        lo, n = rchunks[c]
        cols = pl.ds(lo, n)

        def add(q, j):
            for zz in range(Z):
                G[t, zz, q, :, cols] = (
                    G[t, zz, q, :, cols].astype(F32) + R1[j, zz, :, cols].astype(F32)
                ).astype(BF)

        rs_copy(c, 2).wait_recv()
        add(yx2, 1)
        rs_copy(c, 3).start()
        rs_copy(c, 1).wait_recv()
        add(yx, 0)

    def rs3(c):
        lo, n = rchunks[c]
        cols = pl.ds(lo, n)
        rs_copy(c, 3).wait_recv()
        for zz in range(Z):
            G[t, zz, yx, :, cols] = (
                G[t, zz, yx, :, cols].astype(F32) + R2[zz, :, cols].astype(F32)
            ).astype(BF)
        for kind in (4, 5, 6):
            rs_copy(c, kind).start()

    def rs4(c):
        lo, n = rchunks[c]
        cols = pl.ds(lo, n)
        total = G[t, z, yx, :, cols].astype(F32)
        for kind in (4, 5, 6):
            rs_copy(c, kind).wait_recv()
            total = total + R3[kind - 4, :, cols].astype(F32)
        total = total * s.factor
        if lo < QW:
            for piece in range(n // 128):
                pr, j = (lo // 128 + piece) // 3, (lo // 128 + piece) % 3
                g_qkv[j, :, 128 * pr:128 * pr + 128] = total[:, 128 * piece:128 * piece + 128]
        elif lo == C_OUT:
            g_out[...] = total
        else:
            for piece in range(n // 128):
                col = lo + 128 * piece - (QW + H2W)
                dst = g_dn if (col // FC) % 2 else g_up
                to = (col // (2 * FC)) * FC + col % FC
                dst[:, to:to + 128] = total[:, 128 * piece:128 * piece + 128]

    rs_steps = (rs0, rs1, rs2, rs3, rs4)

    def weight_grad(lhs, rhs, lo, c_lo, n):
        for half in range(2):
            y = nn(lhs[...], rhs[half, :, lo:lo + n])
            G[half, :, :, :, c_lo:c_lo + n] = y.astype(BF).reshape(Z, YX, D // GROUPS, n)
            if c_lo < QW:
                share = y * wl(half, c_lo, n).astype(F32)
                GAINS[...] += sum(share[:, j:j + 128] for j in range(0, n, 128))

    for fc in range(NFC):
        run(s.plan["feed" + str(fc) + "_wait"])
        ag_done("feed" + str(fc) + "_wait")
        feed(fc)
        weight_grad(H2T, GI, fc * FC, c_up(fc), FC)
        run(s.plan["w" + str(2 * fc)])
        weight_grad(COTT, HID, fc * FC, c_dn(fc), FC)
        run(s.plan["w" + str(2 * fc + 1)])

    loop(s.rows // s.big["feed_back"], feed_back, s.plan["feed_back"])
    weight_grad(GBT, O, 0, C_OUT, H2W)
    run(s.plan["out"])

    GP = GI

    def attend_back(pr, i):
        places = [(b, half) for b in range(s.back) for half in range(2)]
        places = [(i * s.back + b, half) for b, half in places]
        grads = [stacked(GO[half, rows_of(b), 128 * pr:128 * pr + 128]) for b, half in places]
        dps = [nt(values_of(half, pr, rows_of(b)), up) for (b, half), up in zip(places, grads)]
        scores = []
        for (b, half), dp in zip(places, dps):
            p = PT[half, b, pr].astype(F32)
            corr = jnp.sum(p * dp, axis=0, keepdims=True)
            scores.append((p * (dp - corr)).astype(BF))
        lo = 384 * pr
        for (b, half), ds in zip(places, scores):
            r = rows_of(b)
            dk = nn(ds, stacked(part_of(half, pr, r, 0)))
            GP[half, r, lo + 128:lo + 256] = dk[:BLK].astype(BF)
            DSV[pr, :, :, 256 * half:256 * half + 128] += dk[BLK:].reshape(2, 8, 128)
        for (b, half), ds in zip(places, scores):
            r = rows_of(b)
            GP[half, r, lo:lo + 128] = beside(tn(keys_of(half, pr, r), ds) * (1.0 / math.sqrt(HD)))
        for (b, half), up in zip(places, grads):
            dv = nn(PT[half, b, pr], up)
            GP[half, rows_of(b), lo + 256:lo + 384] = dv[:BLK].astype(BF)
            DSV[pr, :, :, 256 * half + 128:256 * half + 256] += dv[BLK:].reshape(2, 8, 128)

    span_lane = iota((BLK, 128), 1)

    def dsv_copy(pr):
        return small_copy(3 + pr, DSV.at[pr, 1 - t], DSVR.at[pr], pair)

    def shared(pr):
        dsv_copy(pr).wait_recv()
        SHARE[pr] = (DSV[pr, t] + DSVR[pr]) / own_counts
        lo = 384 * pr

        def spread(b):
            r = rows_of(b)
            column = jnp.sum(jnp.where(span_lane == t * NB + b, SPC[...], 0.0), axis=1, keepdims=True)
            first = column == 0.0
            for half in range(2):
                lanes = slice(256 * half, 256 * half + 256)
                add = jnp.where(first, SHARE[pr, pl.ds(b, 1), lanes], SHARE[pr, pl.ds(NB + b, 1), lanes])
                GP[half, r, lo + 128:lo + 384] = (GP[half, r, lo + 128:lo + 384].astype(F32) + add).astype(BF)

        loop(NB, spread)

    loop(NB // s.back, functools.partial(attend_back, 0), s.plan["back0"])
    dsv_copy(0).start()
    run(s.plan["share0"])
    shared(0)
    weight_grad(H1T, GP, 0, 0, 384)
    run(s.plan["q0"])
    loop(NB // s.back, functools.partial(attend_back, 1), s.plan["back1"])
    dsv_copy(1).start()
    weight_grad(H1T, GP, 384, 384, 128)
    run(s.plan["share1"])
    shared(1)
    weight_grad(H1T, GP, 512, 512, 256)
    run(s.plan["q1"])

    folded = [jnp.sum(GAINS[...].T, axis=0, keepdims=True) / gain1[...]]
    folded += [jnp.sum(ACC[j], axis=0, keepdims=True) for j in range(1, 4)]
    for half in range(2):
        line = jnp.sum(BUACC[half], axis=0, keepdims=True)
        folded += [line[:, j * D:(j + 1) * D] for j in range(F2 // D)]
    SM[0] = jnp.concatenate(folded, axis=0)

    run(s.plan["small"])

    def last(i):
        r = rows_of(i, s.big["last"])
        grad = nt(GP[0, r, 0:QW], wl(0, 0, QW)) + nt(GP[1, r, 0:QW], wl(1, 0, QW))
        unit, inverse = unit_rows(tok[r, :].astype(F32))
        e = grad * gain1[...]
        m1 = jnp.mean(e, axis=-1, keepdims=True)
        m2 = jnp.mean(e * unit, axis=-1, keepdims=True)
        H2[r, :] = (MID[r, :] + inverse * (e - m1 - unit * m2)).astype(BF)

    loop(s.rows // s.big["last"], last, s.plan["last"])
    out_copies = [pltpu.make_async_copy(H2, dtok_out, oc.at[0]), pltpu.make_async_copy(H1, res_out, oc.at[1])]
    out_copies[0].start()

    loop(s.rows // s.big["give"], give, s.plan["give"])
    out_copies[1].start()
    for c in range(len(chunks)):
        for _arrived, starts in gathers[c]:
            for kind in starts:
                ag_copy(c, kind).wait_send()
    bup_copy.wait_send()
    for pr in range(2):
        ksv_copy(pr).wait_send()
        dsv_copy(pr).wait_send()
    early = [e for e in s.plan["end"] if e[0] == "s" or e[2] < 4]
    run(early)
    for c in range(len(rchunks)):
        for kind in range(4):
            rs_copy(c, kind).wait_send()
    run([e for e in s.plan["end"] if e not in early])
    for k in range(1, Z):
        small_copy(7 + k, SM.at[3], SMR.at[3 + (z + Z - k) % Z], zpeers[k - 1]).wait_recv()
    summed = (SMR[3] + SMR[4] + SMR[5] + SMR[6]) * s.factor
    o_gain1[...] = summed[0:1]
    o_gain2[...] = summed[1:2]
    o_bout[...] = summed[2:3]
    o_bdown[...] = summed[3:4]
    for j in range(2 * F2 // D):
        o_bup[:, j * D:(j + 1) * D] = summed[4 + j:5 + j]


    for cp in out_copies:
        cp.wait()
    for c in range(len(rchunks)):
        for kind in range(4, 7):
            rs_copy(c, kind).wait_send()
    for i, who in enumerate((pair, peer3, peer2)):
        exchange(i, who).wait_send()
    for k in range(1, Z):
        small_copy(7 + k, SM.at[3], SMR.at[3 + z], zpeers[k - 1]).wait_send()


def deliver(n, *refs):
    ins, outs, held, (got, sent) = refs[:n], refs[n:2 * n], refs[2 * n:3 * n], refs[3 * n:]
    firsts = [pltpu.make_async_copy(ins[i], held[i], got.at[i]) for i in range(n)]
    seconds = [pltpu.make_async_copy(held[i], outs[i], sent.at[i]) for i in range(n)]
    for cp in firsts:
        cp.start()
    for first, second in zip(firsts, seconds):
        first.wait()
        second.start()
    for cp in seconds:
        cp.wait()


def shards(
    tokens, cotangent, span_ids, gain_one, w_qkv, w_out, b_out, gain_two, w_up, b_up, w_down, b_down
):
    s = Sizes()
    dp = lax.axis_size("dp")
    s.sub = dp // GROUPS
    s.D = tokens.shape[2]
    s.rows = tokens.shape[1]
    s.NB = s.rows // BLK
    s.H2W = w_qkv.shape[2]
    s.F2 = w_up.shape[1]
    s.factor = 1.0 / math.sqrt(dp * lax.axis_size("tensor") * s.rows)
    sub, D, H2W, F2, N, NB = s.sub, s.D, s.H2W, s.F2, s.rows, s.NB
    QW = 3 * H2W
    width = QW + H2W + 2 * F2
    s.FC = 512
    s.FC = 512
    s.big = {'proj': 512, 'feed': 512, 'feed_back': 512, 'last': 512, 'give': 512}
    s.back = 2
    s.ag_chunks = [(0, 384), (384, 384), (768, 1280), (2048, 1024)]
    s.ag_fine = (1, 1, 1, 1)
    s.need = {'second': (0,), 'mid': (1,), 'proj_wait': (2,), 'feed0_wait': (), 'feed1_wait': (3,)}
    s.rs_chunks = [(1024, 512), (1536, 512), (2048, 512), (2560, 512), (768, 256), (0, 384), (384, 128), (512, 256)]
    s.plan = {
        "first": (('a', 0, 0), ('a', 1, 0), ('a', 2, 0), ),
        "second": (('a', 0, 4), ('a', 1, 4), ('a', 0, 1), ('a', 0, 2), ('a', 2, 4), ('a', 0, 3), ('a', 1, 1), ('a', 1, 2), ('a', 0, 5), ('a', 0, 6), ('a', 1, 3), ('a', 0, 7), ('a', 3, 0), ('a', 0, 8), ('a', 2, 1), ('a', 1, 5), ('a', 1, 6), ('a', 1, 7), ('a', 2, 2), ('a', 1, 8), ('a', 0, 9), ('a', 3, 4), ),
        "mid": (('a', 2, 5), ('a', 2, 3), ('a', 1, 9), ('a', 3, 1), ('a', 2, 6), ('a', 3, 2), ),
        "third": (),
        "proj_wait": (('a', 2, 9), ('a', 3, 7), ('a', 3, 8), ),
        "feed0_wait": (),
        "feed1_wait": (),
        "w0": (('r', 0, 0), ),
        "w1": (('r', 1, 0), ),
        "w2": (('r', 2, 0), ),
        "w3": (('r', 3, 0), ),
        "out": (('r', 4, 0), ),
        "share0": (),
        "q0": (('r', 5, 0), ('r', 2, 2), ),
        "share1": (('r', 6, 0), ),
        "q1": (('r', 7, 0), ('r', 4, 2), ),
        "small": (('s', 0, 0), ),
        "end": (('r', 7, 2), ('s', 0, 2), ('r', 2, 4), ('r', 5, 3), ('r', 6, 3), ('r', 7, 3), ('s', 0, 3), ('r', 3, 4), ('r', 4, 4), ('r', 5, 4), ('r', 6, 4), ('r', 7, 4), ),
        "attend": (
            (('a', 2, 7), ('a', 3, 3), ),
            (('a', 2, 8), ('a', 3, 5), ),
            (),
            (('a', 3, 6), ),
        ),
        "proj": (
            (),
            (),
        ),
        "feed0": (
            (('a', 3, 9), ),
            (),
        ),
        "feed1": (
            (('r', 0, 1), ),
            (('r', 1, 1), ),
        ),
        "feed_back": (
            (('r', 0, 2), ('r', 2, 1), ),
            (('r', 3, 1), ('r', 1, 2), ),
        ),
        "back0": (
            (),
            (('r', 0, 3), ('r', 4, 1), ),
        ),
        "back1": (
            (),
            (('r', 3, 2), ('r', 5, 1), ('r', 1, 3), ),
        ),
        "last": (
            (('r', 6, 1), ('r', 0, 4), ('r', 2, 3), ),
            (('r', 3, 3), ('r', 7, 1), ('s', 0, 1), ),
        ),
        "give": (
            (('r', 5, 2), ),
            (('r', 1, 4), ('r', 4, 3), ('r', 6, 2), ),
        ),
    }
    groups = [[a * sub + b for b in range(sub)] for a in range(dp // sub)]
    pieces = [jnp.transpose(w_qkv, (1, 0, 2)), w_out.T, w_up, w_down.T]
    if sub > 1:
        pieces = [
            lax.all_gather(piece, "dp", axis=piece.ndim - 2, tiled=True, axis_index_groups=groups)
            for piece in pieces
        ]
    R = D // GROUPS

    def vm(*shape, dtype=BF):
        return pltpu.VMEM(shape, dtype)

    any_space = pl.BlockSpec(memory_space=pl.ANY)
    in_vmem = pl.BlockSpec(memory_space=pltpu.VMEM)
    results = (
        jax.ShapeDtypeStruct((N, D), BF),
        jax.ShapeDtypeStruct((N, D), BF),
        jax.ShapeDtypeStruct((3, R, H2W), F32),
        jax.ShapeDtypeStruct((R, H2W), F32),
        jax.ShapeDtypeStruct((R, F2), F32),
        jax.ShapeDtypeStruct((R, F2), F32),
        jax.ShapeDtypeStruct((1, D), F32),
        jax.ShapeDtypeStruct((1, D), F32),
        jax.ShapeDtypeStruct((1, D), F32),
        jax.ShapeDtypeStruct((1, D), F32),
        jax.ShapeDtypeStruct((1, 2 * F2), F32),
    )
    out = pl.pallas_call(
        functools.partial(kernel, s),
        out_shape=results,
        in_specs=[any_space] * 12,
        out_specs=[any_space] * 2 + [in_vmem] * 9,
        scratch_shapes=[
            vm(2, Z, YX, R, width),
            vm(2, Z, YX, R, width),
            vm(Z, YX, R, width),
            vm(2, Z, R, width),
            vm(Z, R, width),
            vm(Z - 1, R, width),
            vm(N, D),
            vm(D, N),
            vm(2, N, QW),
            vm(2, NB, 2, BLK + 16, 2 * BLK),
            vm(2, N, H2W),
            vm(N, D, dtype=F32),
            vm(N, D),
            vm(D, N),
            vm(D, N),
            vm(2, N, F2),
            vm(2, N, F2),
            vm(N, D),
            vm(D, N),
            vm(2, 8, F2, dtype=F32),
            vm(2, 2, 8, 512, dtype=F32),
            vm(2, 2, 16, 128),
            vm(2, 2, 16, 128),
            vm(2, 2, 8, 512, dtype=F32),
            vm(2, 8, 512, dtype=F32),
            vm(2, 8, 512, dtype=F32),
            vm(D, 128, dtype=F32),
            vm(BLK, 128, dtype=F32),
            vm(8, N, dtype=F32),
            vm(2, 8, F2, dtype=F32),
            vm(4, 8, D, dtype=F32),
            vm(4, 8, D, dtype=F32),
            vm(7, 8, D, dtype=F32),
            vm(N, D),
            vm(N, D),
            vm(N, D, dtype=F32),
            vm(2, N, H2W),
            vm(2 * NB, BLK, dtype=jnp.int32),
            vm(1, D, dtype=F32),
            vm(1, D, dtype=F32),
            vm(1, D, dtype=F32),
            vm(1, D, dtype=F32),
            vm(1, F2, dtype=F32),
            pltpu.SemaphoreType.DMA((len(s.ag_chunks), 22)),
            pltpu.SemaphoreType.DMA((len(s.ag_chunks), 22)),
            pltpu.SemaphoreType.DMA((len(s.rs_chunks), 7)),
            pltpu.SemaphoreType.DMA((len(s.rs_chunks), 7)),
            pltpu.SemaphoreType.DMA((11,)),
            pltpu.SemaphoreType.DMA((11,)),
            pltpu.SemaphoreType.DMA((24,)),
            pltpu.SemaphoreType.DMA((2,)),
        ],
        compiler_params=pltpu.CompilerParams(
            collective_id=0, has_side_effects=True, vmem_limit_bytes=62 << 20
        ),
    )(
        tokens[0], cotangent[0], span_ids[0], gain_one[None], gain_two[None], b_out[None], b_down[None],
        b_up[None], *pieces,
    )
    out = list(out)
    if sub > 1:
        for i in range(2, 6):
            out[i] = lax.psum_scatter(
                out[i], "dp", scatter_dimension=out[i].ndim - 2, tiled=True, axis_index_groups=groups
            )
        out[6:] = lax.psum(tuple(out[6:]), "dp", axis_index_groups=groups)
    else:
        out = pl.pallas_call(
            functools.partial(deliver, len(results)),
            out_shape=results,
            in_specs=[any_space] * len(results),
            out_specs=[any_space] * len(results),
            scratch_shapes=[pltpu.VMEM(r.shape, r.dtype) for r in results]
            + [pltpu.SemaphoreType.DMA((len(results),))] * 2,
        )(*out)
    result, d_tokens, dq, do, du, dd, g1, g2, bo, bd, bu = out
    return (
        result[None],
        d_tokens[None],
        g1[0],
        jnp.transpose(dq, (1, 0, 2)),
        do.T,
        bo[0],
        g2[0],
        du,
        bu[0],
        dd.T,
        bd[0],
    )


def solution(mesh):
    in_specs = (
        P("dp", "tensor", None),
        P("dp", "tensor", None),
        P("dp", None, None),
        P(),
        P("dp", None, "tensor"),
        P("tensor", "dp"),
        P(),
        P(),
        P("dp", "tensor"),
        P("tensor"),
        P("tensor", "dp"),
        P(),
    )
    out_specs = (
        P("dp", "tensor", None),
        P("dp", "tensor", None),
        P(),
        P("dp", None, "tensor"),
        P("tensor", "dp"),
        P(),
        P(),
        P("dp", "tensor"),
        P(),
        P("tensor", "dp"),
        P(),
    )
    return jax.shard_map(shards, mesh=mesh, in_specs=in_specs, out_specs=out_specs, check_vma=False)
```

```python
import functools
import math

import jax
import jax.numpy as jnp
from jax import lax
from jax.experimental import pallas as pl
from jax.experimental.pallas import tpu as pltpu
from jax.sharding import PartitionSpec as P

HD = 64
BLK = 256
EPS = 1e-05
MASKED = -1e30
Z = 4
YX = 4
GROUPS = Z * YX
F32 = jnp.float32
BF = jnp.bfloat16
MESH = pl.DeviceIdType.MESH


def dot(a, b, ca, cb):
    return lax.dot_general(a, b, (((ca,), (cb,)), ((), ())), preferred_element_type=F32)


def nn(a, b):
    return dot(a, b, 1, 0)


def nt(a, b):
    return dot(a, b, 1, 1)


def tn(a, b):
    return dot(a, b, 0, 0)


def iota(shape, axis):
    return lax.broadcasted_iota(jnp.int32, shape, axis)


def unit_rows(values):
    centre = values - jnp.mean(values, axis=-1, keepdims=True)
    spread = jnp.mean(centre * centre, axis=-1, keepdims=True)
    inverse = lax.rsqrt(spread + EPS)
    return centre * inverse, inverse


def eight(values):
    return jnp.sum(values.reshape(values.shape[0] // 8, 8, values.shape[1]), axis=0)


class Sizes:
    pass


def kernel(s, *refs):
    (tok_in, cot_in, span_in, gain1_in, gain2_in, bout_in, bdown_in, bup_in, s_qkv, s_out, s_up, s_dn) = refs[:12]
    (res_out, dtok_out, g_qkv, g_out, g_up, g_dn, o_gain1, o_gain2, o_bout, o_bdown, o_bup) = refs[12:23]
    (W, G, R0, R1, R2, R3, H1, H1T, QKV, PT, O, MID, H2, H2T, COTT, HID, GI, GB, GBT,
     BUP, KSV, KSB, VSB, DSV, DSVR, SHARE, GAINS, SPC, M8, BUACC, ACC, SM, SMR, tok, cot, RES, GO,
     span, gain1, gain2, bout, bdown, bup_own,
     ag_s, ag_r, rs_s, rs_r, sx_s, sx_r, lc, oc) = refs[23:]
    D, H2W, F2, NB = s.D, s.H2W, s.F2, s.NB
    QW = 3 * H2W
    FC, NFC = s.FC, F2 // s.FC
    C_OUT = QW

    def c_up(fc):
        return QW + H2W + 2 * FC * fc

    def c_dn(fc):
        return QW + H2W + 2 * FC * fc + FC

    d = lax.axis_index("dp")
    t = lax.axis_index("tensor")
    g = d // s.sub
    z = g // YX
    yx = g % YX
    rest = d % s.sub
    b2 = 2 - t
    b3 = 1 + t

    def at(zz, q):
        return ((zz * YX + q) * s.sub + rest, t)

    def flip(q, bit):
        y_bit, x_bit = q // 2, q % 2
        return jnp.where(bit == 2, (1 - y_bit) * 2 + x_bit, y_bit * 2 + 1 - x_bit)

    yx2 = flip(yx, b2)
    yx3 = flip(yx, b3)
    yx23 = 3 - yx
    pair = (d, 1 - t)
    peer2 = at(z, yx2)
    peer3 = at(z, yx3)
    zpeers = [at((z + k) % Z, yx) for k in range(1, Z)]

    barrier = pltpu.get_barrier_semaphore()
    for who in [pair, peer2, peer3] + zpeers:
        pl.semaphore_signal(barrier, inc=1, device_id=who, device_id_type=MESH)

    fetches = []

    def fetch(src, dst):
        cp = pltpu.make_async_copy(src, dst, lc.at[len(fetches)])
        cp.start()
        fetches.append(cp)

    fetch(span_in, span)
    fetch(bup_in, bup_own)
    own = W.at[t, z, yx]
    for j in range(3):
        for pr in range(2):
            fetch(s_qkv.at[j, :, pl.ds(128 * pr, 128)], own.at[:, pl.ds(384 * pr + 128 * j, 128)])
    fetch(s_out, own.at[:, pl.ds(C_OUT, H2W)])
    for fc in range(NFC):
        fetch(s_up.at[:, pl.ds(fc * FC, FC)], own.at[:, pl.ds(c_up(fc), FC)])
        fetch(s_dn.at[:, pl.ds(fc * FC, FC)], own.at[:, pl.ds(c_dn(fc), FC)])
    n_shards = len(fetches)
    for src, dst in ((gain1_in, gain1), (gain2_in, gain2), (bout_in, bout), (bdown_in, bdown)):
        fetch(src, dst)
    fetch(tok_in, tok)
    fetch(cot_in, cot)

    for cp in fetches[2:n_shards]:
        cp.wait()
    pl.semaphore_wait(barrier, 3 + Z - 1)

    def remote(src, dst, ss, rs, who):
        return pltpu.make_async_remote_copy(
            src_ref=src, dst_ref=dst, send_sem=ss, recv_sem=rs, device_id=who, device_id_type=MESH
        )

    chunks = s.ag_chunks
    group_of = {"o": yx, "2": yx2, "3": yx3, "23": yx23}
    kinds = ["z1", "z2", "z3"] + [a + str(k) for a in ("2s", "3s", "3t") for k in range(Z)]
    kinds += ["2g", "3g", "3h"] + ["p" + a for a in group_of]
    number = {kind: i for i, kind in enumerate(kinds)}

    def ag_copy(c, kind, got=False):
        lo, n = chunks[c]
        cols = pl.ds(lo, n)
        if kind[0] == "z":
            k = int(kind[1])
            window, who = W.at[t, (z + Z - k) % Z if got else z, yx, :, cols], zpeers[k - 1]
        elif kind[0] == "p":
            window, who = W.at[1 - t if got else t, :, group_of[kind[1:]], :, cols], pair
        else:
            there, here, who = {
                "2s": (yx2, yx, peer2), "3s": (yx3, yx, peer3), "3t": (yx23, yx2, peer3),
                "2g": (yx2, yx, peer2), "3g": (yx3, yx, peer3), "3h": (yx23, yx2, peer3),
            }[kind[:2]]
            group = there if got else here
            if len(kind) == 2:
                window = W.at[t, :, group, :, cols]
            else:
                window = W.at[t, (z + Z - int(kind[2])) % Z, group, :, cols]
        i = number[kind]
        return remote(window, window, ag_s.at[c, i], ag_r.at[c, i], who)

    def ag_done(place):
        for c in s.need[place]:
            for name in group_of:
                ag_copy(c, "p" + name, True).wait_recv()

    order = (1, 3, 2)
    after = (0, 1, 3, 2)

    def ag_events(fine):
        if not fine:
            return [
                ([], ["z1", "z3", "z2"]),
                (["z1", "z3", "z2"], ["2g", "3g", "po"]),
                (["2g"], ["3h", "p2"]),
                (["3g"], ["p3"]),
                (["3h"], ["p23"]),
            ]
        out = [([], ["z1", "z3", "z2", "2s0", "3s0"])]
        out += [([f"z{k}"], [f"2s{k}", f"3s{k}"] + (["po"] if k == 2 else [])) for k in order]
        out += [([f"2s{k}"], [f"3t{k}"] + (["p2"] if k == 2 else [])) for k in after]
        out += [([f"3s{k}" for k in after], ["p3"]), ([f"3t{k}" for k in after], ["p23"])]
        return out

    gathers = [ag_events(fine) for fine in s.ag_fine]

    def ag_event(c, step):
        arrived, starts = gathers[c][step]
        for kind in arrived:
            ag_copy(c, kind, True).wait_recv()
        for kind in starts:
            ag_copy(c, kind).start()

    def run(events):
        for kind, c, step in events:
            if kind == "a":
                ag_event(c, step)
            elif kind == "r":
                rs_steps[step](c)
            else:
                small_step(step)

    def in_slots(i, places):
        for when, events in enumerate(places):
            if events:
                @pl.when(i == when)
                def _():
                    run(events)

    def small_copy(i, src, dst, who):
        return remote(src, dst, sx_s.at[i], sx_r.at[i], who)

    def exchange(i, who):
        return small_copy(5 + i, SM.at[i], SMR.at[i], who)

    def small_step(i):
        whos = (pair, peer3, peer2)
        if i > 0:
            exchange(i - 1, whos[i - 1]).wait_recv()
            SM[i] = SM[i - 1] + SMR[i - 1]
        if i < 3:
            exchange(i, whos[i]).start()
        else:
            SMR[3 + z] = SM[3]
            for k in range(1, Z):
                small_copy(7 + k, SM.at[3], SMR.at[3 + z], zpeers[k - 1]).start()

    run(s.plan["first"])
    for cp in fetches[:2]:
        cp.wait()
    BUP[t] = jnp.broadcast_to(bup_own[...], (8, F2))
    bup_copy = small_copy(0, BUP.at[t], BUP.at[t], pair)
    bup_copy.start()

    def wl(half, lo, n):
        return W[half, :, :, :, pl.ds(lo, n)].reshape(D, n)

    def rows_of(b, n=BLK):
        return pl.ds(pl.multiple_of(b * n, n), n)

    def loop(count, body, places=()):
        def step(i, _):
            body(i)
            in_slots(i, places)
            return 0

        lax.fori_loop(0, count, step, 0)


    for cp in fetches[n_shards:]:
        cp.wait()

    def norm_one(b, _):
        r = rows_of(b)
        unit, _inv = unit_rows(tok[r, :].astype(F32))
        low = (unit * gain1[...]).astype(BF)
        H1[r, :] = low
        H1T[:, r] = low.T
        COTT[:, r] = cot[r, :].T
        return 0

    lax.fori_loop(0, NB, norm_one, 0)

    half_rows = iota((8, BLK), 0)
    for b in range(NB):
        line = span[pl.ds(t * NB + b, 1), :]
        belongs = jnp.logical_and(half_rows // NB == line, half_rows % NB == b)
        M8[:, b * BLK:(b + 1) * BLK] = belongs.astype(F32)
    SPC[...] = jnp.concatenate([span[...].astype(F32), jnp.zeros((120, BLK), F32)], axis=0).T
    zeros_in = (span[...] == 0).astype(F32)
    ones_in = (span[...] == 1).astype(F32)
    n_zero = jnp.sum(zeros_in, axis=1, keepdims=True)
    n_one = jnp.sum(ones_in, axis=1, keepdims=True)
    counts = jnp.concatenate(
        [n_zero[:NB], n_one[:NB], n_zero[NB:2 * NB], n_one[NB:2 * NB]], axis=0
    )
    log_counts = jnp.log(counts)
    own_counts = jnp.sum(M8[...], axis=1, keepdims=True)
    code = iota((16, 1), 0)
    block_of = (code // 8) * NB + code % NB


    BUACC[...] = jnp.zeros_like(BUACC)
    ACC[...] = jnp.zeros_like(ACC)
    GAINS[...] = jnp.zeros_like(GAINS)
    DSV[...] = jnp.zeros_like(DSV)

    q_scale = jnp.where(iota((1, 384), 1) < 128, 1.0 / math.sqrt(HD), 1.0).astype(F32)
    member_low = jnp.concatenate([M8[...], M8[...]], axis=0).astype(BF)

    def ksv_copy(pr, got=False):
        window = KSV.at[pr, 1 - t if got else t]
        return small_copy(1 + pr, window, window, pair)

    def project(pr):
        lo = 384 * pr
        for half in range(2):
            QKV[half, :, lo:lo + 384] = (nn(H1[...], wl(half, lo, 384)) * q_scale).astype(BF)
        for half in range(2):
            sums = nn(member_low, QKV[half, :, lo + 128:lo + 384])[:8]
            KSV[pr, t, :, 256 * half:256 * half + 256] = (sums / own_counts).astype(BF).astype(F32)
        ksv_copy(pr).start()

    run(s.plan["second"])
    ag_done("second")
    project(0)
    run(s.plan["mid"])
    ag_done("mid")
    project(1)
    run(s.plan["third"])
    for pr in range(2):
        ksv_copy(pr, True).wait_recv()
        everything = KSV[pr].reshape(16, 512).astype(BF)
        for half in range(2):
            KSB[half, pr] = everything[:, 256 * half:256 * half + 128]
            VSB[half, pr] = everything[:, 256 * half + 128:256 * half + 256]

    even = iota((BLK, 128), 1) < HD

    def stacked(values):
        zero = jnp.zeros_like(values)
        return jnp.concatenate([jnp.where(even, values, zero), jnp.where(even, zero, values)], axis=0)

    def beside(values):
        return jnp.concatenate([values[:HD, :BLK], values[HD:, BLK:]], axis=0).astype(BF).T

    def part_of(half, pr, r, which):
        lo = 384 * pr + 128 * which
        return QKV[half, r, lo:lo + 128]

    def keys_of(half, pr, r):
        return jnp.concatenate([part_of(half, pr, r, 1), KSB[half, pr]], axis=0)

    def values_of(half, pr, r):
        return jnp.concatenate([part_of(half, pr, r, 2), VSB[half, pr]], axis=0)

    units = [(half, pr) for half in range(2) for pr in range(2)]

    def attend(b):
        r = rows_of(b)
        seen = block_of < t * NB + b
        scores = [nt(keys_of(half, pr, r), stacked(part_of(half, pr, r, 0))) for half, pr in units]
        probs = []
        for (half, pr), score in zip(units, scores):
            near = score[:BLK]
            far = jnp.where(seen, score[BLK:] + log_counts, MASKED)
            largest = jnp.maximum(jnp.max(near, axis=0, keepdims=True), jnp.max(far, axis=0, keepdims=True))
            near = jnp.exp(near - largest)
            far = jnp.exp(far - largest)
            inv = 1.0 / (jnp.sum(near, axis=0, keepdims=True) + jnp.sum(far, axis=0, keepdims=True))
            low = jnp.concatenate([(near * inv).astype(BF), (far * inv).astype(BF)], axis=0)
            PT[half, b, pr] = low
            probs.append(low)
        for (half, pr), low in zip(units, probs):
            O[half, r, 128 * pr:128 * pr + 128] = beside(tn(values_of(half, pr, r), low))

    loop(NB, attend, s.plan["attend"])

    run(s.plan["proj_wait"])
    ag_done("proj_wait")
    small_copy(0, BUP.at[1 - t], BUP.at[1 - t], pair).wait_recv()

    def out_proj(i):
        r = rows_of(i, s.big["proj"])
        branch = nt(O[0, r, :], wl(0, C_OUT, H2W)) + nt(O[1, r, :], wl(1, C_OUT, H2W))
        middle = tok[r, :].astype(F32) + (branch + bout[...])
        RES[r, :] = middle
        unit, _inv = unit_rows(middle)
        low = (unit * gain2[...]).astype(BF)
        H2[r, :] = low
        H2T[:, r] = low.T

    loop(s.rows // s.big["proj"], out_proj, s.plan["proj"])

    c0 = math.sqrt(2.0 / math.pi)
    c1 = c0 * 0.044715

    def feed(fc):
        cols = slice(fc * FC, (fc + 1) * FC)

        def one(i):
            r = rows_of(i, s.big["feed"])
            for half in range(2):
                x = nn(H2[r, :], wl(half, c_up(fc), FC)) + BUP[half, 0:1, cols]
                gh = nn(cot[r, :], wl(half, c_dn(fc), FC))
                sq = x * x
                th = jnp.tanh(x * (c0 + c1 * sq))
                up = 0.5 + 0.5 * th
                HID[half, r, cols] = (x * up).astype(BF)
                slope = up + (0.5 * x) * (1.0 - th * th) * (c0 + (3.0 * c1) * sq)
                gi = gh * slope
                GI[half, r, cols] = gi.astype(BF)
                BUACC[half, :, cols] += eight(gi)

        loop(s.rows // s.big["feed"], one, s.plan["feed" + str(fc)])

    def over_units(values, r, place):
        total = None
        for half in range(2):
            for fc in range(NFC):
                part = nt(values[half, r, fc * FC:(fc + 1) * FC], wl(half, place(fc), FC))
                total = part if total is None else total + part
        return total

    def feed_back(i):
        r = rows_of(i, s.big["feed_back"])
        g2 = over_units(GI, r, c_up)
        unit, inverse = unit_rows(RES[r, :])
        e = g2 * gain2[...]
        m1 = jnp.mean(e, axis=-1, keepdims=True)
        m2 = jnp.mean(e * unit, axis=-1, keepdims=True)
        grad_out = cot[r, :].astype(F32)
        mid = grad_out + inverse * (e - m1 - unit * m2)
        MID[r, :] = mid
        low = mid.astype(BF)
        GB[r, :] = low
        GBT[:, r] = low.T
        for half in range(2):
            GO[half, r, :] = nn(low, wl(half, C_OUT, H2W)).astype(BF)
        ACC[1] += eight(g2 * unit)
        ACC[2] += eight(mid)
        ACC[3] += eight(grad_out)

    def give(i):
        r = rows_of(i, s.big["give"])
        H1[r, :] = (RES[r, :] + (over_units(HID, r, c_dn) + bdown[...])).astype(BF)

    rchunks = s.rs_chunks

    def rs_copy(c, kind):
        lo, n = rchunks[c]
        cols = pl.ds(lo, n)
        if kind == 0:
            src, dst, who = G.at[1 - t, :, :, :, cols], R0.at[:, :, :, cols], pair
        elif kind == 1:
            src, dst, who = G.at[t, :, yx3, :, cols], R1.at[0, :, :, cols], peer3
        elif kind == 2:
            src, dst, who = G.at[t, :, yx23, :, cols], R1.at[1, :, :, cols], peer3
        elif kind == 3:
            src, dst, who = G.at[t, :, yx2, :, cols], R2.at[:, :, cols], peer2
        else:
            k = kind - 3
            src, dst, who = G.at[t, (z + k) % Z, yx, :, cols], R3.at[k - 1, :, cols], zpeers[k - 1]
        return remote(src, dst, rs_s.at[c, kind], rs_r.at[c, kind], who)

    def rs0(c):
        rs_copy(c, 0).start()

    def rs1(c):
        lo, n = rchunks[c]
        rs_copy(c, 0).wait_recv()
        cols = pl.ds(lo, n)

        def add(q):
            for zz in range(Z):
                G[t, zz, q, :, cols] = (
                    G[t, zz, q, :, cols].astype(F32) + R0[zz, q, :, cols].astype(F32)
                ).astype(BF)

        add(yx23)
        rs_copy(c, 2).start()
        add(yx3)
        rs_copy(c, 1).start()
        add(yx2)
        add(yx)

    def rs2(c):
        lo, n = rchunks[c]
        cols = pl.ds(lo, n)

        def add(q, j):
            for zz in range(Z):
                G[t, zz, q, :, cols] = (
                    G[t, zz, q, :, cols].astype(F32) + R1[j, zz, :, cols].astype(F32)
                ).astype(BF)

        rs_copy(c, 2).wait_recv()
        add(yx2, 1)
        rs_copy(c, 3).start()
        rs_copy(c, 1).wait_recv()
        add(yx, 0)

    def rs3(c):
        lo, n = rchunks[c]
        cols = pl.ds(lo, n)
        rs_copy(c, 3).wait_recv()
        for zz in range(Z):
            G[t, zz, yx, :, cols] = (
                G[t, zz, yx, :, cols].astype(F32) + R2[zz, :, cols].astype(F32)
            ).astype(BF)
        for kind in (4, 5, 6):
            rs_copy(c, kind).start()

    def rs4(c):
        lo, n = rchunks[c]
        cols = pl.ds(lo, n)
        total = G[t, z, yx, :, cols].astype(F32)
        for kind in (4, 5, 6):
            rs_copy(c, kind).wait_recv()
            total = total + R3[kind - 4, :, cols].astype(F32)
        total = total * s.factor
        if lo < QW:
            for piece in range(n // 128):
                pr, j = (lo // 128 + piece) // 3, (lo // 128 + piece) % 3
                g_qkv[j, :, 128 * pr:128 * pr + 128] = total[:, 128 * piece:128 * piece + 128]
        elif lo == C_OUT:
            g_out[...] = total
        else:
            for piece in range(n // 128):
                col = lo + 128 * piece - (QW + H2W)
                dst = g_dn if (col // FC) % 2 else g_up
                to = (col // (2 * FC)) * FC + col % FC
                dst[:, to:to + 128] = total[:, 128 * piece:128 * piece + 128]

    rs_steps = (rs0, rs1, rs2, rs3, rs4)

    def weight_grad(lhs, rhs, lo, c_lo, n):
        for half in range(2):
            y = nn(lhs[...], rhs[half, :, lo:lo + n])
            G[half, :, :, :, c_lo:c_lo + n] = y.astype(BF).reshape(Z, YX, D // GROUPS, n)
            if c_lo < QW:
                share = y * wl(half, c_lo, n).astype(F32)
                GAINS[...] += sum(share[:, j:j + 128] for j in range(0, n, 128))

    for fc in range(NFC):
        run(s.plan["feed" + str(fc) + "_wait"])
        ag_done("feed" + str(fc) + "_wait")
        feed(fc)
        weight_grad(H2T, GI, fc * FC, c_up(fc), FC)
        run(s.plan["w" + str(2 * fc)])
        weight_grad(COTT, HID, fc * FC, c_dn(fc), FC)
        run(s.plan["w" + str(2 * fc + 1)])

    loop(s.rows // s.big["feed_back"], feed_back, s.plan["feed_back"])
    weight_grad(GBT, O, 0, C_OUT, H2W)
    run(s.plan["out"])

    GP = GI

    def attend_back(pr, i):
        places = [(b, half) for b in range(s.back) for half in range(2)]
        places = [(i * s.back + b, half) for b, half in places]
        grads = [stacked(GO[half, rows_of(b), 128 * pr:128 * pr + 128]) for b, half in places]
        dps = [nt(values_of(half, pr, rows_of(b)), up) for (b, half), up in zip(places, grads)]
        scores = []
        for (b, half), dp in zip(places, dps):
            p = PT[half, b, pr].astype(F32)
            corr = jnp.sum(p * dp, axis=0, keepdims=True)
            scores.append((p * (dp - corr)).astype(BF))
        lo = 384 * pr
        for (b, half), ds in zip(places, scores):
            r = rows_of(b)
            dk = nn(ds, stacked(part_of(half, pr, r, 0)))
            GP[half, r, lo + 128:lo + 256] = dk[:BLK].astype(BF)
            DSV[pr, :, :, 256 * half:256 * half + 128] += dk[BLK:].reshape(2, 8, 128)
        for (b, half), ds in zip(places, scores):
            r = rows_of(b)
            GP[half, r, lo:lo + 128] = beside(tn(keys_of(half, pr, r), ds) * (1.0 / math.sqrt(HD)))
        for (b, half), up in zip(places, grads):
            dv = nn(PT[half, b, pr], up)
            GP[half, rows_of(b), lo + 256:lo + 384] = dv[:BLK].astype(BF)
            DSV[pr, :, :, 256 * half + 128:256 * half + 256] += dv[BLK:].reshape(2, 8, 128)

    span_lane = iota((BLK, 128), 1)

    def dsv_copy(pr):
        return small_copy(3 + pr, DSV.at[pr, 1 - t], DSVR.at[pr], pair)

    def shared(pr):
        dsv_copy(pr).wait_recv()
        SHARE[pr] = (DSV[pr, t] + DSVR[pr]) / own_counts
        lo = 384 * pr

        def spread(b):
            r = rows_of(b)
            column = jnp.sum(jnp.where(span_lane == t * NB + b, SPC[...], 0.0), axis=1, keepdims=True)
            first = column == 0.0
            for half in range(2):
                lanes = slice(256 * half, 256 * half + 256)
                add = jnp.where(first, SHARE[pr, pl.ds(b, 1), lanes], SHARE[pr, pl.ds(NB + b, 1), lanes])
                GP[half, r, lo + 128:lo + 384] = (GP[half, r, lo + 128:lo + 384].astype(F32) + add).astype(BF)

        loop(NB, spread)

    loop(NB // s.back, functools.partial(attend_back, 0), s.plan["back0"])
    dsv_copy(0).start()
    run(s.plan["share0"])
    shared(0)
    weight_grad(H1T, GP, 0, 0, 384)
    run(s.plan["q0"])
    loop(NB // s.back, functools.partial(attend_back, 1), s.plan["back1"])
    dsv_copy(1).start()
    weight_grad(H1T, GP, 384, 384, 128)
    run(s.plan["share1"])
    shared(1)
    weight_grad(H1T, GP, 512, 512, 256)
    run(s.plan["q1"])

    folded = [jnp.sum(GAINS[...].T, axis=0, keepdims=True) / gain1[...]]
    folded += [jnp.sum(ACC[j], axis=0, keepdims=True) for j in range(1, 4)]
    for half in range(2):
        line = jnp.sum(BUACC[half], axis=0, keepdims=True)
        folded += [line[:, j * D:(j + 1) * D] for j in range(F2 // D)]
    SM[0] = jnp.concatenate(folded, axis=0)

    run(s.plan["small"])

    def last(i):
        r = rows_of(i, s.big["last"])
        grad = nt(GP[0, r, 0:QW], wl(0, 0, QW)) + nt(GP[1, r, 0:QW], wl(1, 0, QW))
        unit, inverse = unit_rows(tok[r, :].astype(F32))
        e = grad * gain1[...]
        m1 = jnp.mean(e, axis=-1, keepdims=True)
        m2 = jnp.mean(e * unit, axis=-1, keepdims=True)
        H2[r, :] = (MID[r, :] + inverse * (e - m1 - unit * m2)).astype(BF)

    loop(s.rows // s.big["last"], last, s.plan["last"])
    out_copies = [pltpu.make_async_copy(H2, dtok_out, oc.at[0]), pltpu.make_async_copy(H1, res_out, oc.at[1])]
    out_copies[0].start()

    loop(s.rows // s.big["give"], give, s.plan["give"])
    out_copies[1].start()
    for c in range(len(chunks)):
        for _arrived, starts in gathers[c]:
            for kind in starts:
                ag_copy(c, kind).wait_send()
    bup_copy.wait_send()
    for pr in range(2):
        ksv_copy(pr).wait_send()
        dsv_copy(pr).wait_send()
    early = [e for e in s.plan["end"] if e[0] == "s" or e[2] < 4]
    run(early)
    for c in range(len(rchunks)):
        for kind in range(4):
            rs_copy(c, kind).wait_send()
    run([e for e in s.plan["end"] if e not in early])
    for k in range(1, Z):
        small_copy(7 + k, SM.at[3], SMR.at[3 + (z + Z - k) % Z], zpeers[k - 1]).wait_recv()
    summed = (SMR[3] + SMR[4] + SMR[5] + SMR[6]) * s.factor
    o_gain1[...] = summed[0:1]
    o_gain2[...] = summed[1:2]
    o_bout[...] = summed[2:3]
    o_bdown[...] = summed[3:4]
    for j in range(2 * F2 // D):
        o_bup[:, j * D:(j + 1) * D] = summed[4 + j:5 + j]


    for cp in out_copies:
        cp.wait()
    for c in range(len(rchunks)):
        for kind in range(4, 7):
            rs_copy(c, kind).wait_send()
    for i, who in enumerate((pair, peer3, peer2)):
        exchange(i, who).wait_send()
    for k in range(1, Z):
        small_copy(7 + k, SM.at[3], SMR.at[3 + z], zpeers[k - 1]).wait_send()


def deliver(n, *refs):
    ins, outs, held, (got, sent) = refs[:n], refs[n:2 * n], refs[2 * n:3 * n], refs[3 * n:]
    pieces = []
    for i in range(n):
        rows = ins[i].shape[0]
        cuts = 4 if rows >= 4 * BLK else 1
        for j in range(cuts):
            pieces.append((i, pl.ds(j * (rows // cuts), rows // cuts)))
    firsts = [
        pltpu.make_async_copy(ins[i].at[w], held[i].at[w], got.at[k]) for k, (i, w) in enumerate(pieces)
    ]
    seconds = [
        pltpu.make_async_copy(held[i].at[w], outs[i].at[w], sent.at[k]) for k, (i, w) in enumerate(pieces)
    ]
    for cp in firsts:
        cp.start()
    for first, second in zip(firsts, seconds):
        first.wait()
        second.start()
    for cp in seconds:
        cp.wait()


def shards(
    tokens, cotangent, span_ids, gain_one, w_qkv, w_out, b_out, gain_two, w_up, b_up, w_down, b_down
):
    s = Sizes()
    dp = lax.axis_size("dp")
    s.sub = dp // GROUPS
    s.D = tokens.shape[2]
    s.rows = tokens.shape[1]
    s.NB = s.rows // BLK
    s.H2W = w_qkv.shape[2]
    s.F2 = w_up.shape[1]
    s.factor = 1.0 / math.sqrt(dp * lax.axis_size("tensor") * s.rows)
    sub, D, H2W, F2, N, NB = s.sub, s.D, s.H2W, s.F2, s.rows, s.NB
    QW = 3 * H2W
    width = QW + H2W + 2 * F2
    s.FC = 512
    s.FC = 512
    s.big = {'proj': 512, 'feed': 512, 'feed_back': 512, 'last': 512, 'give': 512}
    s.back = 2
    s.ag_chunks = [(0, 384), (384, 384), (768, 1280), (2048, 1024)]
    s.ag_fine = (1, 1, 1, 1)
    s.need = {'second': (0,), 'mid': (1,), 'proj_wait': (2,), 'feed0_wait': (), 'feed1_wait': (3,)}
    s.rs_chunks = [(1024, 512), (1536, 512), (2048, 512), (2560, 512), (768, 256), (0, 384), (384, 128), (512, 256)]
    s.plan = {
        "first": (('a', 0, 0), ('a', 1, 0), ('a', 2, 0), ),
        "second": (('a', 0, 4), ('a', 1, 4), ('a', 0, 1), ('a', 0, 2), ('a', 2, 4), ('a', 0, 3), ('a', 1, 1), ('a', 1, 2), ('a', 0, 5), ('a', 0, 6), ('a', 1, 3), ('a', 0, 7), ('a', 3, 0), ('a', 0, 8), ('a', 2, 1), ('a', 1, 5), ('a', 1, 6), ('a', 1, 7), ('a', 2, 2), ('a', 1, 8), ('a', 0, 9), ('a', 3, 4), ),
        "mid": (('a', 2, 5), ('a', 2, 3), ('a', 1, 9), ('a', 3, 1), ('a', 2, 6), ('a', 3, 2), ),
        "third": (),
        "proj_wait": (('a', 2, 9), ('a', 3, 7), ('a', 3, 8), ),
        "feed0_wait": (),
        "feed1_wait": (),
        "w0": (('r', 0, 0), ),
        "w1": (('r', 1, 0), ),
        "w2": (('r', 2, 0), ),
        "w3": (('r', 3, 0), ),
        "out": (('r', 4, 0), ),
        "share0": (),
        "q0": (('r', 5, 0), ('r', 2, 2), ),
        "share1": (('r', 6, 0), ),
        "q1": (('r', 7, 0), ('r', 4, 2), ),
        "small": (('s', 0, 0), ),
        "end": (('r', 7, 2), ('s', 0, 2), ('r', 2, 4), ('r', 5, 3), ('r', 6, 3), ('r', 7, 3), ('s', 0, 3), ('r', 3, 4), ('r', 4, 4), ('r', 5, 4), ('r', 6, 4), ('r', 7, 4), ),
        "attend": (
            (('a', 2, 7), ('a', 3, 3), ),
            (('a', 2, 8), ('a', 3, 5), ),
            (),
            (('a', 3, 6), ),
        ),
        "proj": (
            (),
            (),
        ),
        "feed0": (
            (('a', 3, 9), ),
            (),
        ),
        "feed1": (
            (('r', 0, 1), ),
            (('r', 1, 1), ),
        ),
        "feed_back": (
            (('r', 0, 2), ('r', 2, 1), ),
            (('r', 3, 1), ('r', 1, 2), ),
        ),
        "back0": (
            (),
            (('r', 0, 3), ('r', 4, 1), ),
        ),
        "back1": (
            (),
            (('r', 3, 2), ('r', 5, 1), ('r', 1, 3), ),
        ),
        "last": (
            (('r', 6, 1), ('r', 0, 4), ('r', 2, 3), ),
            (('r', 3, 3), ('r', 7, 1), ('s', 0, 1), ),
        ),
        "give": (
            (('r', 5, 2), ),
            (('r', 1, 4), ('r', 4, 3), ('r', 6, 2), ),
        ),
    }
    groups = [[a * sub + b for b in range(sub)] for a in range(dp // sub)]
    pieces = [jnp.transpose(w_qkv, (1, 0, 2)), w_out.T, w_up, w_down.T]
    if sub > 1:
        pieces = [
            lax.all_gather(piece, "dp", axis=piece.ndim - 2, tiled=True, axis_index_groups=groups)
            for piece in pieces
        ]
    R = D // GROUPS

    def vm(*shape, dtype=BF):
        return pltpu.VMEM(shape, dtype)

    any_space = pl.BlockSpec(memory_space=pl.ANY)
    in_vmem = pl.BlockSpec(memory_space=pltpu.VMEM)
    results = (
        jax.ShapeDtypeStruct((N, D), BF),
        jax.ShapeDtypeStruct((N, D), BF),
        jax.ShapeDtypeStruct((3, R, H2W), F32),
        jax.ShapeDtypeStruct((R, H2W), F32),
        jax.ShapeDtypeStruct((R, F2), F32),
        jax.ShapeDtypeStruct((R, F2), F32),
        jax.ShapeDtypeStruct((1, D), F32),
        jax.ShapeDtypeStruct((1, D), F32),
        jax.ShapeDtypeStruct((1, D), F32),
        jax.ShapeDtypeStruct((1, D), F32),
        jax.ShapeDtypeStruct((1, 2 * F2), F32),
    )
    out = pl.pallas_call(
        functools.partial(kernel, s),
        out_shape=results,
        in_specs=[any_space] * 12,
        out_specs=[any_space] * 2 + [in_vmem] * 9,
        scratch_shapes=[
            vm(2, Z, YX, R, width),
            vm(2, Z, YX, R, width),
            vm(Z, YX, R, width),
            vm(2, Z, R, width),
            vm(Z, R, width),
            vm(Z - 1, R, width),
            vm(N, D),
            vm(D, N),
            vm(2, N, QW),
            vm(2, NB, 2, BLK + 16, 2 * BLK),
            vm(2, N, H2W),
            vm(N, D, dtype=F32),
            vm(N, D),
            vm(D, N),
            vm(D, N),
            vm(2, N, F2),
            vm(2, N, F2),
            vm(N, D),
            vm(D, N),
            vm(2, 8, F2, dtype=F32),
            vm(2, 2, 8, 512, dtype=F32),
            vm(2, 2, 16, 128),
            vm(2, 2, 16, 128),
            vm(2, 2, 8, 512, dtype=F32),
            vm(2, 8, 512, dtype=F32),
            vm(2, 8, 512, dtype=F32),
            vm(D, 128, dtype=F32),
            vm(BLK, 128, dtype=F32),
            vm(8, N, dtype=F32),
            vm(2, 8, F2, dtype=F32),
            vm(4, 8, D, dtype=F32),
            vm(4, 8, D, dtype=F32),
            vm(7, 8, D, dtype=F32),
            vm(N, D),
            vm(N, D),
            vm(N, D, dtype=F32),
            vm(2, N, H2W),
            vm(2 * NB, BLK, dtype=jnp.int32),
            vm(1, D, dtype=F32),
            vm(1, D, dtype=F32),
            vm(1, D, dtype=F32),
            vm(1, D, dtype=F32),
            vm(1, F2, dtype=F32),
            pltpu.SemaphoreType.DMA((len(s.ag_chunks), 22)),
            pltpu.SemaphoreType.DMA((len(s.ag_chunks), 22)),
            pltpu.SemaphoreType.DMA((len(s.rs_chunks), 7)),
            pltpu.SemaphoreType.DMA((len(s.rs_chunks), 7)),
            pltpu.SemaphoreType.DMA((11,)),
            pltpu.SemaphoreType.DMA((11,)),
            pltpu.SemaphoreType.DMA((24,)),
            pltpu.SemaphoreType.DMA((2,)),
        ],
        compiler_params=pltpu.CompilerParams(
            collective_id=0, has_side_effects=True, vmem_limit_bytes=62 << 20
        ),
    )(
        tokens[0], cotangent[0], span_ids[0], gain_one[None], gain_two[None], b_out[None], b_down[None],
        b_up[None], *pieces,
    )
    out = list(out)
    if sub > 1:
        for i in range(2, 6):
            out[i] = lax.psum_scatter(
                out[i], "dp", scatter_dimension=out[i].ndim - 2, tiled=True, axis_index_groups=groups
            )
        out[6:] = lax.psum(tuple(out[6:]), "dp", axis_index_groups=groups)
    else:
        out = pl.pallas_call(
            functools.partial(deliver, len(results)),
            out_shape=results,
            in_specs=[any_space] * len(results),
            out_specs=[any_space] * len(results),
            scratch_shapes=[pltpu.VMEM(r.shape, r.dtype) for r in results]
            + [pltpu.SemaphoreType.DMA((len(results) + 6,))] * 2,
        )(*out)
    result, d_tokens, dq, do, du, dd, g1, g2, bo, bd, bu = out
    return (
        result[None],
        d_tokens[None],
        g1[0],
        jnp.transpose(dq, (1, 0, 2)),
        do.T,
        bo[0],
        g2[0],
        du,
        bu[0],
        dd.T,
        bd[0],
    )


def solution(mesh):
    in_specs = (
        P("dp", "tensor", None),
        P("dp", "tensor", None),
        P("dp", None, None),
        P(),
        P("dp", None, "tensor"),
        P("tensor", "dp"),
        P(),
        P(),
        P("dp", "tensor"),
        P("tensor"),
        P("tensor", "dp"),
        P(),
    )
    out_specs = (
        P("dp", "tensor", None),
        P("dp", "tensor", None),
        P(),
        P("dp", None, "tensor"),
        P("tensor", "dp"),
        P(),
        P(),
        P("dp", "tensor"),
        P(),
        P("tensor", "dp"),
        P(),
    )
    return jax.shard_map(shards, mesh=mesh, in_specs=in_specs, out_specs=out_specs, check_vma=False)
```
